32 devices in a mesh: head: 2 (over y), tm: 16 (over z, x, core).
Axes of the slice: x: 2, y: 2, z: 4, core: 2. Of those that a mesh axis runs over, the one named last changes fastest.
Arguments:
- frames: bfloat16 [16384, 1024], P('tm'), may hold values from -6 to 6
- segment_lengths: int32 [128], replicated, may hold values from 1 to 512, 16384 in all
- attn_gain: float32 [1024], replicated, may hold values from 0.5 to 1.5
- qkv_proj: bfloat16 [1024, 3, 1024], P('tm', None, 'head'), may hold values from -0.1875 to 0.1875
- out_proj: bfloat16 [1024, 1024], P(None, 'tm'), may hold values from -0.1875 to 0.1875
- logit_scale: float32 [16], P('head'), may hold values from 2 to 16
- conv_gain: float32 [1024], replicated, may hold values from 0.5 to 1.5
- glu_proj: bfloat16 [1024, 2048], P('tm'), may hold values from -0.1875 to 0.1875
- kernel: float32 [31, 1024], replicated, may hold values from -1 to 1
- post_gain: float32 [1024], replicated, may hold values from 0.5 to 1.5
- mix_proj: bfloat16 [1024, 1024], P('tm'), may hold values from -0.1875 to 0.1875
- cotangent: bfloat16 [16384, 1024], P('tm', 'head'), may hold values from -6 to 6
Outputs:
- out_frames: bfloat16 [16384, 1024], P('tm', 'head')
- grad_input: bfloat16 [16384, 1024], P('tm', 'head')
- grad_kernel: float32 [31, 1024], replicated
- grad_gains: float32 [2, 1024], replicated
The draws below stay inside these ranges and needn't reach their ends.
Inputs may be any that keep to these rules, and one draw needn't show every extreme that they name: `segment_lengths`: the 128 lengths sum to 16384; the longest is exactly 512 frames.
All inputs are finite; a program needn't handle non-finite values.
Results may differ from the reference program's by a relative error of at most 0.014.
Values may be sent and summed in bfloat16 or wider, within the bound.
No kernel may reach another device: no remote copies, remote signals or barrier semaphores. Data moves between devices by JAX's collectives and lax.ppermute only.
A program may use at most 128 MiB of HBM per device.

```python
import math
import jax
import jax.numpy as jnp
import numpy as np
from jax import lax

D = 1024
HEADS = 16
HD = 64
KERNEL = 31
HALF = 15
TOK_DEV = 1024
TOKENS = 16384
MOST = 512
SEGS = 128


def levels(key, dims, split, least, top_value):
    factor_of, own = 1.0, jax.random.fold_in(key, 6)
    for position, blocks in split:
        heights = jnp.exp(jax.random.uniform(jax.random.fold_in(own, position), (blocks,), jnp.float32, least / len(split), top_value / len(split)))
        factor_of = factor_of * jnp.repeat(heights, dims[position] // blocks).reshape([-1 if axis == position else 1 for axis in range(len(dims))])
    return factor_of


def profile(amount, total, limit, skew):
    portions = [(1 << 20) // math.isqrt(grade ** skew) + 1 for grade in range(2, amount + 1)]
    surplus, counts = total - limit - (amount - 1), [1] * (amount - 1)
    while surplus > 0:
        free = [i for i in range(amount - 1) if counts[i] < limit]
        mass, budget = sum([portions[i] for i in free]), surplus
        for i in free:
            addition = min(limit - counts[i], max(1, budget * portions[i] // mass), surplus)
            counts[i] = counts[i] + addition
            surplus = surplus - addition
    return np.array([limit] + counts)


def uneven(key, number_of, total, most, slope):
    if number_of == 2:
        one = jax.random.randint(key, (), max(1, total - most), min(most, total - 1) + 1)
        return jnp.stack([one, total - one])
    lengths = jnp.asarray(profile(number_of, total, most, slope), jnp.int32)
    twos = (number_of - 1) // 2
    donor, sink = lengths[1:1 + 2 * twos:2], lengths[2:2 + 2 * twos:2]
    room = jnp.minimum(donor - 1, most - sink)
    shifted = jax.random.randint(jax.random.fold_in(key, 1), (twos,), 0, 1 << 20) % (room + 1)
    lengths = lengths.at[1:1 + 2 * twos:2].set(donor - shifted).at[2:2 + 2 * twos:2].set(sink + shifted)
    return lengths[jax.random.permutation(jax.random.fold_in(key, 2), number_of)]


def normal_values(stream_key, dims, scale, limit, shards=(), kind=jnp.bfloat16):
    loudness = levels(stream_key, dims, shards, -0.22, 0.18) if shards else 1.0
    result = jax.random.normal(stream_key, dims, jnp.float32) * scale * loudness
    return jnp.minimum(jnp.maximum(result, -limit), limit).astype(kind)


def setup_inputs(seed: int = 0) -> dict:
    key_list = jax.random.split(jax.random.key(seed), 13)
    frames = normal_values(key_list[0], (TOKENS, D), 1.0, 6.0, ((0, 16),))
    segment_lengths = uneven(key_list[1], SEGS, TOKENS, MOST, 2).astype(jnp.int32)
    attn_gain = jnp.clip(1.0 + 0.1 * jax.random.normal(key_list[2], (D,), jnp.float32), 0.5, 1.5)
    qkv_proj = normal_values(key_list[3], (D, 3, D), D ** -0.5, 0.1875, ((0, 16), (2, 2)))
    out_proj = normal_values(key_list[4], (D, D), D ** -0.5, 0.1875, ((1, 16),))
    logit_scale = jnp.clip(jnp.exp(math.log(16.0) - 2.0794415 * jax.random.uniform(key_list[5], (HEADS,), jnp.float32) ** levels(key_list[5], (HEADS,), ((0, 2),), -0.2, 0.2)), 2.0, 16.0)
    conv_gain = jnp.clip(1.0 + 0.1 * jax.random.normal(key_list[6], (D,), jnp.float32), 0.5, 1.5)
    glu_proj = normal_values(key_list[7], (D, 2 * D), D ** -0.5, 0.1875, ((0, 16),))
    kernel = normal_values(key_list[8], (KERNEL, D), KERNEL ** -0.5, 1.0, (), jnp.float32)
    post_gain = jnp.clip(1.0 + 0.1 * jax.random.normal(key_list[9], (D,), jnp.float32), 0.5, 1.5)
    mix_proj = normal_values(key_list[10], (D, D), D ** -0.5, 0.1875, ((0, 16),))
    cotangent = normal_values(key_list[11], (TOKENS, D), 1.0, 6.0, ((0, 16), (1, 2)))
    return dict(frames=frames, segment_lengths=segment_lengths, attn_gain=attn_gain, qkv_proj=qkv_proj, out_proj=out_proj, logit_scale=logit_scale, conv_gain=conv_gain, glu_proj=glu_proj, kernel=kernel, post_gain=post_gain, mix_proj=mix_proj, cotangent=cotangent)


EPS_NORM = 1e-05
EPS_HEAD = 1e-06

def layer_stats(values):
    average = lax.optimization_barrier(jnp.mean(values, axis=-1, keepdims=True))
    centred = values - average
    inverse = lax.rsqrt(lax.optimization_barrier(jnp.mean(centred * centred, axis=-1, keepdims=True)) + EPS_NORM)
    return (centred * inverse, inverse)

def unit_heads(values):
    return values * lax.rsqrt(lax.optimization_barrier(jnp.mean(values * values, axis=-1, keepdims=True)) + EPS_HEAD)

def norm_back(gradient, normed, inverse, gain):
    scaled = gradient * gain
    return inverse * (scaled - lax.optimization_barrier(jnp.mean(scaled, axis=-1, keepdims=True)) - normed * lax.optimization_barrier(jnp.mean(scaled * normed, axis=-1, keepdims=True)))

def segment_of(segment_lengths, positions):
    segment_ends = jnp.cumsum(segment_lengths).astype(jnp.int32)
    located = jnp.searchsorted(segment_ends, positions, side='right').astype(jnp.int32)
    return jnp.where(positions < 0, -1, located).astype(jnp.int32)

def reference(frames, segment_lengths, attn_gain, qkv_proj, out_proj, logit_scale, conv_gain, glu_proj, kernel, post_gain, mix_proj, cotangent):
    all_frames = frames.shape[0]
    model_width = frames.shape[1]
    frame_float = frames.astype(jnp.float32)
    attn_normed = (layer_stats(frame_float)[0] * attn_gain).astype(jnp.bfloat16)
    projected = jnp.dot(attn_normed, qkv_proj.reshape(model_width, 3 * model_width), preferred_element_type=jnp.float32)
    query_heads = unit_heads(projected[:, :model_width].reshape(all_frames, HEADS, HD)).astype(jnp.bfloat16)
    key_heads = unit_heads(projected[:, model_width:2 * model_width].reshape(all_frames, HEADS, HD)).astype(jnp.bfloat16)
    value_heads = projected[:, 2 * model_width:].astype(jnp.bfloat16).reshape(all_frames, HEADS, HD)
    margin = jnp.zeros((MOST, HEADS, HD), jnp.bfloat16)
    key_padded = jnp.concatenate([margin, key_heads, margin], 0)
    value_padded = jnp.concatenate([margin, value_heads, margin], 0)
    key_segment = segment_of(segment_lengths, jnp.arange(-MOST, all_frames + MOST, dtype=jnp.int32))
    query_block = min(512, TOK_DEV)
    window = query_block + 2 * MOST
    factor = (logit_scale / HD)[:, None, None]

    def attend_block(block_index):
        row_start = (block_index * query_block).astype(jnp.int32)
        query_rows = lax.dynamic_slice_in_dim(query_heads, row_start, query_block, 0).astype(jnp.float32)
        key_rows = lax.dynamic_slice_in_dim(key_padded, row_start, window, 0).astype(jnp.float32)
        value_rows = lax.dynamic_slice_in_dim(value_padded, row_start, window, 0).astype(jnp.float32)
        query_seg = lax.dynamic_slice_in_dim(key_segment, row_start + MOST, query_block, 0)
        key_seg = lax.dynamic_slice_in_dim(key_segment, row_start, window, 0)
        scores = jnp.einsum('qhd,khd->hqk', query_rows, key_rows) * factor
        weights = jnp.where((query_seg[:, None] == key_seg[None, :])[None], jnp.exp(scores), 0.0)
        weights = (weights / lax.optimization_barrier(jnp.sum(weights, axis=-1, keepdims=True))).astype(jnp.bfloat16)
        mixed_heads = jnp.einsum('hqk,khd->qhd', weights.astype(jnp.float32), value_rows)
        return mixed_heads.astype(jnp.bfloat16).reshape(query_block, model_width)
    heads_out = lax.map(attend_block, jnp.arange(all_frames // query_block, dtype=jnp.int32)).reshape(all_frames, model_width)
    residual = (frame_float + jnp.dot(heads_out, out_proj, preferred_element_type=jnp.float32)).astype(jnp.bfloat16)
    residual_float = residual.astype(jnp.float32)
    conv_normed, conv_inverse = layer_stats(residual_float)
    conv_input = (conv_normed * conv_gain).astype(jnp.bfloat16)
    glu_linear = jnp.dot(conv_input, glu_proj, preferred_element_type=jnp.float32)
    glu_value = glu_linear[:, :model_width]
    gate_sigmoid = jax.nn.sigmoid(glu_linear[:, model_width:])
    gated = (glu_value * gate_sigmoid).astype(jnp.bfloat16)
    rim_zeros = jnp.zeros((HALF, model_width), jnp.bfloat16)
    gated_padded = jnp.concatenate([rim_zeros, gated, rim_zeros], 0)
    conv_segment = segment_of(segment_lengths, jnp.arange(-HALF, all_frames + HALF, dtype=jnp.int32))
    centre = conv_segment[HALF:HALF + all_frames]
    tap_masks = [(conv_segment[offset:offset + all_frames] == centre).astype(jnp.float32)[:, None] for offset in range(KERNEL)]
    depth_out = jnp.zeros((all_frames, model_width), jnp.float32)
    for offset in range(KERNEL):
        depth_out = depth_out + kernel[offset] * gated_padded[offset:offset + all_frames].astype(jnp.float32) * tap_masks[offset]
    post_normed, post_inverse = layer_stats(depth_out)
    post_scaled = post_normed * post_gain
    post_sigmoid = jax.nn.sigmoid(post_scaled)
    swished = (post_scaled * post_sigmoid).astype(jnp.bfloat16)
    out_frames = (residual_float + jnp.dot(swished, mix_proj, preferred_element_type=jnp.float32)).astype(jnp.bfloat16)
    swish_grad = jnp.dot(cotangent, mix_proj.T, preferred_element_type=jnp.float32)
    post_grad = swish_grad * (post_sigmoid * (1.0 + post_scaled * (1.0 - post_sigmoid)))
    depth_grad = norm_back(post_grad, post_normed, post_inverse, post_gain).astype(jnp.bfloat16)
    depth_padded = jnp.concatenate([rim_zeros, depth_grad, rim_zeros], 0)
    depth_float = depth_grad.astype(jnp.float32)
    gated_grad = jnp.zeros((all_frames, model_width), jnp.float32)
    kernel_terms = []
    for offset in range(KERNEL):
        gated_grad = gated_grad + kernel[KERNEL - 1 - offset] * depth_padded[offset:offset + all_frames].astype(jnp.float32) * tap_masks[offset]
        kernel_terms.append(lax.optimization_barrier(jnp.sum(depth_float * gated_padded[offset:offset + all_frames].astype(jnp.float32) * tap_masks[offset], axis=0)))
    glu_grad = jnp.concatenate([gated_grad * gate_sigmoid, gated_grad * glu_value * gate_sigmoid * (1.0 - gate_sigmoid)], 1).astype(jnp.bfloat16)
    input_grad = jnp.dot(glu_grad, glu_proj.T, preferred_element_type=jnp.float32)
    grad_input = (cotangent.astype(jnp.float32) + norm_back(input_grad, conv_normed, conv_inverse, conv_gain)).astype(jnp.bfloat16)
    grad_scale = 1.0 / math.sqrt(all_frames)
    grad_kernel = jnp.stack(kernel_terms, 0) * grad_scale
    grad_gains = jnp.stack([lax.optimization_barrier(jnp.sum(input_grad * conv_normed, axis=0)), lax.optimization_barrier(jnp.sum(post_grad * post_normed, axis=0))], 0) * grad_scale
    return (out_frames, grad_input, grad_kernel, grad_gains)
```

```python
import functools
import math

import jax
import jax.numpy as jnp
from jax import lax
from jax.experimental import pallas as pl
from jax.experimental.pallas import tpu as pltpu
from jax.sharding import PartitionSpec as P

HD = 64
KERNEL = 31
HALF = 15
MOST = 512
LANE = 128
PAD = 64
RIM = 32
EDGE = 16
KEYS = 256

EPS_NORM = 1e-05
EPS_HEAD = 1e-06


F32 = jnp.float32
BF16 = jnp.bfloat16
VMEM_SPEC = pl.BlockSpec(memory_space=pltpu.VMEM)
ANY_SPEC = pl.BlockSpec(memory_space=pl.ANY)
SMEM_SPEC = pl.BlockSpec(memory_space=pltpu.SMEM)


def tile_of(count, most):
    best = 16
    for size in range(16, most + 1, 16):
        if count % size == 0:
            best = size
    return best


def dot_nn(a, b):
    return lax.dot_general(a, b, (((1,), (0,)), ((), ())), preferred_element_type=F32)


def dot_nt(a, b):
    return lax.dot_general(a, b, (((1,), (1,)), ((), ())), preferred_element_type=F32)


def row_stats(values):
    average = jnp.mean(values, axis=-1, keepdims=True)
    centred = values - average
    inverse = lax.rsqrt(jnp.mean(centred * centred, axis=-1, keepdims=True) + EPS_NORM)
    return centred * inverse, inverse


def slot_copies(ids_ref, halves, target, sems, column=0):
    slots = ids_ref.shape[0]
    each = slots // len(halves)
    rows = target.shape[0] // slots
    columns = pl.ds(column, target.shape[1])
    copies = []
    for slot in range(slots):
        source = halves[slot // each].at[pl.ds((slot % each) * rows, rows), columns]
        place = pl.multiple_of(ids_ref[slot] * rows, rows)
        copies.append(
            pltpu.make_async_copy(source, target.at[pl.ds(place, rows), :], sems.at[slot])
        )
    return copies


def start_all(copies):
    for copy in copies:
        copy.start()


def wait_all(copies):
    for copy in copies:
        copy.wait()


def cost(flops, moved):
    return pl.CostEstimate(flops=flops, transcendentals=0, bytes_accessed=moved)


def norm_kernel(places_ref, gain_ref, *refs):
    out_ref = refs[-1]
    for piece, ref in enumerate(refs[:-1]):
        place = places_ref[piece]
        chunk = tile_of(ref.shape[0], 96)

        def step(index, carry, ref=ref, place=place, chunk=chunk):
            start = pl.multiple_of(index * chunk, chunk)
            normed, _ = row_stats(ref[pl.ds(start, chunk), :].astype(F32))
            target = pl.multiple_of(place + start, chunk)
            out_ref[pl.ds(target, chunk), :] = (normed * gain_ref[...]).astype(BF16)
            return carry

        lax.fori_loop(0, ref.shape[0] // chunk, step, 0)


def norm_rows(places, gain, pieces):
    rows = sum(piece.shape[0] for piece in pieces)
    width = pieces[0].shape[1]
    return pl.pallas_call(
        norm_kernel,
        grid_spec=pltpu.PrefetchScalarGridSpec(
            num_scalar_prefetch=1,
            grid=(1,),
            in_specs=[VMEM_SPEC] * (1 + len(pieces)),
            out_specs=VMEM_SPEC,
        ),
        out_shape=jax.ShapeDtypeStruct((rows, width), BF16),
        cost_estimate=cost(0, 12 * rows * width),
        name="norm_rows",
    )(places, gain, *pieces)


def qkv_kernel(ids_ref, alt_ref, x_ref, ka, kb, va, vb, qa, qb, scale_ref, *refs):
    k_out, v_out, q_out, k_weight, v_weight, q_weight, k_sems, v_sems, q_sems = refs
    first = pl.program_id(0) == 0
    k_copies = slot_copies(ids_ref, (ka, kb), k_weight, k_sems)
    v_copies = slot_copies(ids_ref, (va, vb), v_weight, v_sems)
    q_copies = slot_copies(alt_ref, (qa, qb), q_weight, q_sems)

    @pl.when(first)
    def _():
        start_all(k_copies + v_copies + q_copies)
        wait_all(k_copies)

    x = x_ref[...]
    width = k_weight.shape[1]
    group = min(KEYS, width)
    row_head = lax.broadcasted_iota(jnp.int32, (group, group), 0) // HD
    column_head = lax.broadcasted_iota(jnp.int32, (group, group), 1) // HD
    ones = jnp.where(row_head == column_head, 1.0, 0.0).astype(BF16)

    def unit(product, out, scale):
        for start in range(0, width, group):
            part = product[:, start : start + group]
            total = dot_nn((part * part).astype(BF16), ones)
            scaled = part * lax.rsqrt(total * (1.0 / HD) + EPS_HEAD)
            if scale is not None:
                scaled = scaled * scale[:, start : start + group]
            out[:, start : start + group] = scaled.astype(BF16)

    unit(dot_nn(x, k_weight[...]), k_out, None)

    @pl.when(first)
    def _():
        wait_all(v_copies)

    v_out[...] = dot_nn(x, v_weight[...]).astype(BF16)

    @pl.when(first)
    def _():
        wait_all(q_copies)

    unit(dot_nn(x, q_weight[...]), q_out, scale_ref)


def project(ids, alternate, x, key_halves, value_halves, query_halves, scale):
    rows, width = x.shape
    columns = key_halves[0].shape[1]
    slots = ids.shape[0]
    tile = tile_of(rows, 544)
    row_spec = pl.BlockSpec((tile, columns), lambda i, a, b: (i, 0))
    return pl.pallas_call(
        qkv_kernel,
        grid_spec=pltpu.PrefetchScalarGridSpec(
            num_scalar_prefetch=2,
            grid=(rows // tile,),
            in_specs=[pl.BlockSpec((tile, width), lambda i, a, b: (i, 0))]
            + [ANY_SPEC] * 6
            + [pl.BlockSpec((1, columns), lambda i, a, b: (0, 0))],
            out_specs=[row_spec] * 3,
            scratch_shapes=[pltpu.VMEM((width, columns), BF16)] * 3
            + [pltpu.SemaphoreType.DMA((slots,))] * 3,
        ),
        out_shape=[jax.ShapeDtypeStruct((rows, columns), BF16)] * 3,
        cost_estimate=cost(12 * rows * width * columns, 12 * width * width),
        name="project",
    )(ids, alternate, x, *key_halves, *value_halves, *query_halves, scale)


def attend_kernel(
    first_ref, count_ref, q_ref, k_ref, v_ref, qseg_ref, kseg_ref, out_ref, acc_ref, bias_ref
):
    block = pl.program_id(0)
    rows, width = q_ref.shape
    lane = lax.broadcasted_iota(jnp.int32, (rows, LANE), 1)
    lane_keys = lax.broadcasted_iota(jnp.int32, (KEYS, LANE), 1)
    acc_ref[...] = jnp.zeros_like(acc_ref)
    query_segment = qseg_ref[...]

    def step(index, carry):
        start = pl.multiple_of(first_ref[block] + index * KEYS, LANE)
        same = query_segment == kseg_ref[:, pl.ds(start, KEYS)]
        bias_ref[...] = jnp.where(same, 0.0, -1e30)
        for pair in range(width // LANE):
            columns = pl.ds(pair * LANE, LANE)
            queries = q_ref[:, columns]
            keys = k_ref[pl.ds(start, KEYS), columns]
            values = v_ref[pl.ds(start, KEYS), columns]
            for side in range(2):
                mine = (lane < HD) if side == 0 else (lane >= HD)
                mine_keys = (lane_keys < HD) if side == 0 else (lane_keys >= HD)
                one = jnp.where(mine, queries, jnp.zeros_like(queries))
                scores = dot_nt(one, keys) + bias_ref[...]
                weights = jnp.exp2(scores).astype(BF16)
                extended = jnp.where(mine_keys, values, jnp.ones_like(values))
                acc_ref[2 * pair + side] += dot_nn(weights, extended)
        return carry

    lax.fori_loop(0, count_ref[block], step, 0)
    for pair in range(width // LANE):
        even, odd = acc_ref[2 * pair], acc_ref[2 * pair + 1]
        above = jnp.where(lane < HD, even, odd)
        below = pltpu.roll(jnp.where(lane < HD, odd, even), HD, 1)
        out_ref[:, pl.ds(pair * LANE, LANE)] = (above / below).astype(BF16)


def attend(first, count, queries, keys, values, query_segment, key_segment):
    width = queries.shape[1]
    key_rows = keys.shape[0]
    rows = query_segment.shape[0]
    block = rows // first.shape[0]
    return pl.pallas_call(
        attend_kernel,
        grid_spec=pltpu.PrefetchScalarGridSpec(
            num_scalar_prefetch=2,
            grid=(rows // block,),
            in_specs=[
                pl.BlockSpec((block, width), lambda i, a, b: (i, 0)),
                pl.BlockSpec((key_rows, width), lambda i, a, b: (0, 0)),
                pl.BlockSpec((key_rows, width), lambda i, a, b: (0, 0)),
                pl.BlockSpec((block, 1), lambda i, a, b: (i, 0)),
                pl.BlockSpec((1, key_rows), lambda i, a, b: (0, 0)),
            ],
            out_specs=pl.BlockSpec((block, width), lambda i, a, b: (i, 0)),
            scratch_shapes=[
                pltpu.VMEM((width // HD, block, LANE), F32),
                pltpu.VMEM((block, KEYS), F32),
            ],
        ),
        out_shape=jax.ShapeDtypeStruct((rows, width), BF16),
        cost_estimate=cost(16 * rows * width * width, 20 * rows * width),
        name="attend",
    )(first, count, queries, keys, values, query_segment, key_segment)


def open_kernel(
    parts, ids_ref, alt_ref, place_ref, *refs
):
    heads_refs = refs[:parts]
    (frames_ref, gain_ref, one_a, one_b, two_a, two_b) = refs[parts : parts + 6]
    (res_ref, gated_ref, value_ref, gate_ref) = refs[parts + 6 : parts + 10]
    out_weight, value_weight, gate_weight, out_sems, value_sems, gate_sems = refs[parts + 10 :]

    width = frames_ref.shape[1]
    first = pl.program_id(0) == 0
    out_copies = slot_copies(ids_ref, (one_a, one_b), out_weight, out_sems)
    glu_copies = slot_copies(ids_ref, (one_a, one_b), value_weight, value_sems, width)
    glu_copies += slot_copies(alt_ref, (two_a, two_b), gate_weight, gate_sems)

    @pl.when(first)
    def _():
        start_all(out_copies + glu_copies)
        wait_all(out_copies)

    heads = jnp.concatenate([ref[0] for ref in heads_refs], axis=1)
    total = frames_ref[...].astype(F32) + dot_nt(heads, out_weight[...])
    residual = total.astype(BF16)
    res_ref[...] = residual
    normed, _ = row_stats(residual.astype(F32))
    conv_input = (normed * gain_ref[...]).astype(BF16)

    @pl.when(first)
    def _():
        wait_all(glu_copies)

    value = dot_nn(conv_input, value_weight[...])
    gate = jax.nn.sigmoid(dot_nn(conv_input, gate_weight[...]))
    value_ref[...] = value
    gate_ref[...] = gate
    gated_ref[...] = (value * gate).astype(BF16)


def open_block(ids, alternate, places, heads, frames, gain, one_halves, two_halves):
    parts, rows, local = heads.shape
    width = frames.shape[1]
    tile = tile_of(rows, 288)
    slots = ids.shape[0]

    def head_spec(source):
        return pl.BlockSpec((1, tile, local), lambda i, a, b, place: (place[source], i, 0))

    row_spec = pl.BlockSpec((tile, width), lambda i, a, b, place: (i, 0))
    return pl.pallas_call(
        functools.partial(open_kernel, parts),
        grid_spec=pltpu.PrefetchScalarGridSpec(
            num_scalar_prefetch=3,
            grid=(rows // tile,),
            in_specs=[head_spec(s) for s in range(parts)]
            + [row_spec, pl.BlockSpec((1, width), lambda i, a, b, place: (0, 0))]
            + [ANY_SPEC] * 4,
            out_specs=[row_spec] * 4,
            scratch_shapes=[
                pltpu.VMEM((width, width), BF16),
                pltpu.VMEM((width, width), BF16),
                pltpu.VMEM((width, width), BF16),
                pltpu.SemaphoreType.DMA((slots,)),
                pltpu.SemaphoreType.DMA((slots,)),
                pltpu.SemaphoreType.DMA((slots,)),
            ],
        ),
        out_shape=[
            jax.ShapeDtypeStruct((rows, width), BF16),
            jax.ShapeDtypeStruct((rows, width), BF16),
            jax.ShapeDtypeStruct((rows, width), F32),
            jax.ShapeDtypeStruct((rows, width), F32),
        ],
        cost_estimate=cost(10 * rows * width * width, 24 * rows * width),
        name="open_block",
    )(ids, alternate, places, *([heads] * parts), frames, gain, *one_halves, *two_halves)


SUB = 8
STEP = 8
SPAN = STEP + KERNEL - 1
LEAD = 16


def at_frame(frame, frames=1, tile=SUB):
    start = frame * tile
    if not isinstance(start, int):
        start = pl.multiple_of(start, SUB)
    return pl.ds(start, frames * tile)


def to_frames(source_ref, target, count, shift):
    width = source_ref.shape[1]
    tile = width // LANE

    def step(index, carry):
        start = pl.multiple_of(index * 16, 16)
        for block in range(tile):
            values = source_ref[pl.ds(start, 16), block * LANE : (block + 1) * LANE].astype(F32)
            target[pl.ds((start + shift) * tile + block, 16, stride=tile), :] = values
        return carry

    lax.fori_loop(0, count // 16, step, 0)


def copy_frames(source, target, first, place, count, tile):
    def step(index, carry):
        source_at = at_frame(first + index * STEP, STEP, tile)
        target[at_frame(place + index * STEP, STEP, tile), :] = source[source_at, :]
        return carry

    lax.fori_loop(0, (count + STEP - 1) // STEP, step, 0)


def deal(rows_ref, out_refs, place_ref, start):
    parts = len(out_refs)
    rows, width = rows_ref.shape
    local = width // parts
    for shift, out_ref in enumerate(out_refs):
        head = lax.rem(place_ref[0] + shift, parts)
        columns = pl.ds(pl.multiple_of(head * local, local), local)
        out_ref[pl.ds(start, rows), :] = rows_ref[:, columns]


def middle_kernel(parts, ids_ref, place_ref, limits_ref, *refs):
    up_refs = refs[:parts]
    (gated_ref, res_ref, taps_ref, gain_ref, mix_a, mix_b) = refs[parts : parts + 6]
    out_refs = refs[parts + 6 : 2 * parts + 6]
    (grad_ref, gain_out) = refs[2 * parts + 6 : 2 * parts + 8]
    (cells, buffer, depth, back, swished, mix, turned, sems) = refs[2 * parts + 8 :]
    rows, width = gated_ref.shape
    blocks = width // LANE
    inner = rows - 2 * EDGE
    own = rows - 2 * RIM

    copies = slot_copies(ids_ref, (mix_a, mix_b), mix, sems, width)
    start_all(copies)

    depth[...] = jnp.zeros_like(depth)
    buffer[at_frame(0, LEAD, blocks), :] = jnp.zeros((LEAD * blocks, LANE), F32)
    to_frames(gated_ref, cells, rows, 0)
    segments = limits_ref.shape[0] - 3

    def segment_step(segment, carry):
        first, last = limits_ref[segment], limits_ref[segment + 1]
        length = last - first
        copy_frames(cells, buffer, first, LEAD, length, blocks)
        zeros = jnp.zeros(((LEAD + STEP) * blocks, LANE), F32)
        buffer[at_frame(LEAD + length, LEAD + STEP, blocks), :] = zeros

        def convolve(index, carry):
            start = index * STEP
            sums = [None] * STEP
            for near in range(SPAN):
                frame = buffer[at_frame(start + LEAD - HALF + near, 1, blocks), :]
                for one in range(STEP):
                    tap = near - one
                    if 0 <= tap < KERNEL:
                        term = taps_ref[tap * blocks : (tap + 1) * blocks, :] * frame
                        sums[one] = term if sums[one] is None else sums[one] + term
            for one in range(STEP):
                depth[at_frame(first + start + one, 1, blocks), :] = sums[one]
            return carry

        lax.fori_loop(0, (length + STEP - 1) // STEP, convolve, 0)
        return carry

    lax.fori_loop(limits_ref[segments + 1], limits_ref[segments + 2], segment_step, 0)

    wait_all(copies)

    big = tile_of(inner, 288)

    def backward(index, carry):
        start = pl.multiple_of(index * big, 16)
        upstream = jnp.concatenate(
            [ref[0, pl.ds(start + EDGE, big), :] for ref in up_refs], axis=1
        )
        back[pl.ds(start, big), :] = dot_nt(upstream, mix[...])
        return carry

    lax.fori_loop(0, inner // big, backward, 0)
    gain_out[...] = jnp.zeros_like(gain_out)

    def pointwise(index, carry):
        start = pl.multiple_of(index * 16, 16)
        cuts = [slice(b * LANE, (b + 1) * LANE) for b in range(blocks)]
        values = [
            depth[pl.ds((start + EDGE) * blocks + b, 16, stride=blocks), :] for b in range(blocks)
        ]
        average = jnp.sum(functools.reduce(jnp.add, values), axis=1, keepdims=True) / width
        values = [v - average for v in values]
        spread_of = (
            jnp.sum(functools.reduce(jnp.add, [v * v for v in values]), axis=1, keepdims=True)
            / width
        )
        inverse = lax.rsqrt(spread_of + EPS_NORM)
        scaled, first_sum, second_sum = [], 0.0, 0.0
        is_own = jnp.where((index >= 1) & (index < 1 + own // 16), 1.0, 0.0)
        for b in range(blocks):
            normed = values[b] * inverse
            post = normed * gain_ref[:, cuts[b]]
            gate = jax.nn.sigmoid(post)
            swished[pl.ds(start, 16), cuts[b]] = (post * gate).astype(BF16)
            grad = back[pl.ds(start, 16), cuts[b]] * (gate * (1.0 + post * (1.0 - gate)))
            term = grad * normed
            gain_out[:, cuts[b]] += (term[:8] + term[8:]) * is_own
            part = grad * gain_ref[:, cuts[b]]
            scaled.append(part)
            first_sum = first_sum + part
            second_sum = second_sum + part * normed
            values[b] = normed
        first_mean = jnp.sum(first_sum, axis=1, keepdims=True) / width
        second_mean = jnp.sum(second_sum, axis=1, keepdims=True) / width
        for b in range(blocks):
            grad_ref[pl.ds(start, 16), cuts[b]] = (
                inverse * (scaled[b] - first_mean - values[b] * second_mean)
            ).astype(BF16)
        return carry

    lax.fori_loop(0, inner // 16, pointwise, 0)

    big = tile_of(own, 256)

    def forward(index, carry):
        start = pl.multiple_of(index * big, 16)
        product = dot_nn(swished[pl.ds(start + EDGE, big), :], mix[...])
        turned[...] = (res_ref[pl.ds(start + RIM, big), :].astype(F32) + product).astype(BF16)
        deal(turned, out_refs, place_ref, start)
        return carry

    lax.fori_loop(0, own // big, forward, 0)


def middle_block(ids, places, limits, upstream, gated, residual, taps, gain, mix_halves):
    parts, rows, local = upstream.shape
    width = gated.shape[1]
    slots = ids.shape[0]
    inner, own = rows - 2 * EDGE, rows - 2 * RIM
    blocks = width // LANE

    def up_spec(source):
        return pl.BlockSpec((1, rows, local), lambda i, a, place, b: (place[source], 0, 0))

    return pl.pallas_call(
        functools.partial(middle_kernel, parts),
        grid_spec=pltpu.PrefetchScalarGridSpec(
            num_scalar_prefetch=3,
            grid=(1,),
            in_specs=[up_spec(s) for s in range(parts)] + [VMEM_SPEC] * 4 + [ANY_SPEC] * 2,
            out_specs=[VMEM_SPEC] * (parts + 2),
            scratch_shapes=[
                pltpu.VMEM(((rows + STEP) * blocks, LANE), F32),
                pltpu.VMEM(((rows + 2 * LEAD + STEP) * blocks, LANE), F32),
                pltpu.VMEM(((rows + STEP) * blocks, LANE), F32),
                pltpu.VMEM((inner, width), F32),
                pltpu.VMEM((inner, width), BF16),
                pltpu.VMEM((width, width), BF16),
                pltpu.VMEM((tile_of(own, 256), width), BF16),
                pltpu.SemaphoreType.DMA((slots,)),
            ],
        ),
        out_shape=[jax.ShapeDtypeStruct((own, width // parts), BF16)] * parts
        + [
            jax.ShapeDtypeStruct((inner, width), BF16),
            jax.ShapeDtypeStruct((8, width), F32),
        ],
        cost_estimate=cost(4 * rows * width * width, 60 * rows * width),
        name="middle_block",
    )(ids, places, limits, *([upstream] * parts), gated, residual, taps, gain, *mix_halves)


def spread_kernel(
    limits_ref, grad_ref, gated_ref, value_ref, gate_ref, taps_ref, out_ref, taps_out,
    cells, inputs, buffer, held, total,
):
    rows, width = gated_ref.shape
    blocks = width // LANE
    inner, own = rows - 2 * EDGE, rows - 2 * RIM
    taps_out[...] = jnp.zeros_like(taps_out)
    total[...] = jnp.zeros_like(total)
    buffer[at_frame(0, LEAD, blocks), :] = jnp.zeros((LEAD * blocks, LANE), F32)
    to_frames(grad_ref, cells, inner, EDGE)
    to_frames(gated_ref, inputs, rows, 0)
    segments = limits_ref.shape[0] - 3

    def segment_step(segment, carry):
        first, last = limits_ref[segment], limits_ref[segment + 1]
        own_first, own_last = jnp.maximum(first, RIM), jnp.minimum(last, rows - RIM)
        first, last = jnp.maximum(first, EDGE), jnp.minimum(last, rows - EDGE)

        @pl.when(own_last > own_first)
        def _():
            length, own_length = last - first, own_last - own_first
            skip = own_first - first
            copy_frames(cells, buffer, first, LEAD, length, blocks)
            zeros = jnp.zeros(((LEAD + STEP) * blocks, LANE), F32)
            buffer[at_frame(LEAD + length, LEAD + STEP, blocks), :] = zeros
            copy_frames(inputs, held, own_first, 0, own_length, blocks)
            held[at_frame(own_length, STEP, blocks), :] = jnp.zeros((STEP * blocks, LANE), F32)

            def convolve(index, carry):
                start = index * STEP
                sums = [None] * STEP
                mine = [held[at_frame(start + one, 1, blocks), :] for one in range(STEP)]
                terms = [None] * KERNEL
                for near in range(SPAN):
                    frame = buffer[at_frame(start + skip + LEAD - HALF + near, 1, blocks), :]
                    for one in range(STEP):
                        tap = one + KERNEL - 1 - near
                        if 0 <= tap < KERNEL:
                            place = slice(tap * blocks, (tap + 1) * blocks)
                            term = taps_ref[place, :] * frame
                            sums[one] = term if sums[one] is None else sums[one] + term
                            term = mine[one] * frame
                            terms[tap] = term if terms[tap] is None else terms[tap] + term
                    done = KERNEL - 1 + STEP - 1 - near
                    if 0 <= done < KERNEL:
                        taps_out[done * blocks : (done + 1) * blocks, :] += terms[done]
                for one in range(STEP):
                    total[at_frame(own_first + start + one, 1, blocks), :] = sums[one]
                return carry

            lax.fori_loop(0, (own_length + STEP - 1) // STEP, convolve, 0)

        return carry

    lax.fori_loop(limits_ref[segments + 1], limits_ref[segments + 2], segment_step, 0)

    def gates(index, carry):
        start = pl.multiple_of(index * 16, 16)
        for block in range(blocks):
            columns = slice(block * LANE, (block + 1) * LANE)
            gate = gate_ref[pl.ds(start + RIM, 16), columns]
            value = value_ref[pl.ds(start + RIM, 16), columns]
            through = total[pl.ds((start + RIM) * blocks + block, 16, stride=blocks), :] * gate
            out_ref[pl.ds(start, 16), columns] = through.astype(BF16)
            out_ref[pl.ds(start, 16), width + block * LANE : width + (block + 1) * LANE] = (
                through * value * (1.0 - gate)
            ).astype(BF16)
        return carry

    lax.fori_loop(0, own // 16, gates, 0)


def spread_block(limits, grad, gated, value, gate, taps):
    rows, width = gated.shape
    inner, own = rows - 2 * EDGE, rows - 2 * RIM
    blocks = width // LANE
    return pl.pallas_call(
        spread_kernel,
        grid_spec=pltpu.PrefetchScalarGridSpec(
            num_scalar_prefetch=1,
            grid=(1,),
            in_specs=[VMEM_SPEC] * 5,
            out_specs=[VMEM_SPEC] * 2,
            scratch_shapes=[
                pltpu.VMEM(((rows + STEP) * blocks, LANE), F32),
                pltpu.VMEM(((rows + STEP) * blocks, LANE), F32),
                pltpu.VMEM(((rows + 2 * LEAD + STEP) * blocks, LANE), F32),
                pltpu.VMEM(((own + 2 * STEP) * blocks, LANE), F32),
                pltpu.VMEM(((rows + STEP) * blocks, LANE), F32),
            ],
        ),
        out_shape=[
            jax.ShapeDtypeStruct((own, 2 * width), BF16),
            jax.ShapeDtypeStruct((KERNEL * blocks, LANE), F32),
        ],
        cost_estimate=cost(0, 70 * own * width),
        name="spread_block",
    )(limits, grad, gated, value, gate, taps)


def close_kernel(parts, ids_ref, alt_ref, place_ref, *refs):
    up_refs = refs[:parts]
    (grad_ref, res_ref, gain_ref, one_a, one_b, two_a, two_b) = refs[parts : parts + 7]
    out_refs = refs[parts + 7 : 2 * parts + 7]
    gain_out = refs[2 * parts + 7]
    (value_weight, gate_weight, turned, value_sems, gate_sems) = refs[2 * parts + 8 :]
    own, width = grad_ref.shape[0], res_ref.shape[1]
    copies = slot_copies(ids_ref, (one_a, one_b), value_weight, value_sems, width)
    copies += slot_copies(alt_ref, (two_a, two_b), gate_weight, gate_sems)
    start_all(copies)
    wait_all(copies)
    gain_out[...] = jnp.zeros_like(gain_out)
    tile = tile_of(own, 128)

    def step(index, carry):
        start = pl.multiple_of(index * tile, 16)
        grad = dot_nt(grad_ref[pl.ds(start, tile), :width], value_weight[...])
        grad = grad + dot_nt(grad_ref[pl.ds(start, tile), width:], gate_weight[...])
        normed, inverse = row_stats(res_ref[pl.ds(start + RIM, tile), :].astype(F32))
        term = grad * normed
        gain_out[...] += jnp.sum(term.reshape(tile // 8, 8, width), axis=0)
        scaled = grad * gain_ref[...]
        result = inverse * (
            scaled
            - jnp.mean(scaled, axis=-1, keepdims=True)
            - normed * jnp.mean(scaled * normed, axis=-1, keepdims=True)
        )
        upstream = jnp.concatenate(
            [ref[0, pl.ds(start + RIM, tile), :] for ref in up_refs], axis=1
        ).astype(F32)
        turned[...] = (upstream + result).astype(BF16)
        deal(turned, out_refs, place_ref, start)
        return carry

    lax.fori_loop(0, own // tile, step, 0)


def close_block(ids, alternate, places, upstream, grad, residual, gain, one_halves, two_halves):
    parts, rows, local = upstream.shape
    own, width = grad.shape[0], residual.shape[1]
    slots = ids.shape[0]

    def up_spec(source):
        return pl.BlockSpec((1, rows, local), lambda i, a, b, place: (place[source], 0, 0))

    return pl.pallas_call(
        functools.partial(close_kernel, parts),
        grid_spec=pltpu.PrefetchScalarGridSpec(
            num_scalar_prefetch=3,
            grid=(1,),
            in_specs=[up_spec(s) for s in range(parts)] + [VMEM_SPEC] * 3 + [ANY_SPEC] * 4,
            out_specs=[VMEM_SPEC] * (parts + 1),
            scratch_shapes=[
                pltpu.VMEM((width, width), BF16),
                pltpu.VMEM((width, width), BF16),
                pltpu.VMEM((tile_of(own, 128), width), BF16),
                pltpu.SemaphoreType.DMA((slots,)),
                pltpu.SemaphoreType.DMA((slots,)),
            ],
        ),
        out_shape=[jax.ShapeDtypeStruct((own, width // parts), BF16)] * parts
        + [jax.ShapeDtypeStruct((8, width), F32)],
        cost_estimate=cost(4 * own * width * width, 30 * own * width),
        name="close_block",
    )(
        ids,
        alternate,
        places,
        *([upstream] * parts),
        grad,
        residual,
        gain,
        *one_halves,
        *two_halves,
    )


def after(value, *others):
    return lax.optimization_barrier((value,) + others)[0]


def flip(cells, bit):
    count = lax.axis_size("tm")
    return lax.ppermute(cells, "tm", [(i, i ^ bit) for i in range(count)])


def grow(cells, bit, *others):
    return jnp.concatenate([cells, flip(after(cells, *others), bit)], axis=0)


def slot_order(bits):
    order = []
    for slot in range(lax.axis_size("tm")):
        order.append(sum(bit for level, bit in enumerate(bits) if (slot >> level) & 1))
    return lax.axis_index("tm").astype(jnp.int32) ^ jnp.asarray(order, jnp.int32)


def tm_pairs():
    count = lax.axis_size("tm")
    pairs = []
    for i in range(1, count - 1, 2):
        pairs += [(i, i + 1), (i + 1, i)]
    return pairs


def to_heads(pieces):
    count = lax.axis_size("head")
    me = lax.axis_index("head")
    return send_heads([pieces((me + shift) % count) for shift in range(count)])


def send_heads(pieces):
    count = lax.axis_size("head")
    result = [pieces[0]]
    for shift in range(1, count):
        result.append(
            lax.ppermute(pieces[shift], "head", [(i, (i + shift) % count) for i in range(count)])
        )
    return result


def in_order(parts):
    count = len(parts)
    me = lax.axis_index("head")
    if count == 2:
        return jnp.where(
            me == 0,
            jnp.concatenate(parts, axis=0),
            jnp.concatenate(parts[::-1], axis=0),
        )
    stacked = jnp.stack(parts, 0)
    ordered = jnp.take(stacked, (me - jnp.arange(count)) % count, axis=0)
    return ordered.reshape((-1,) + parts[0].shape[1:])


def on_device(
    frames,
    segment_lengths,
    attn_gain,
    qkv_proj,
    out_proj,
    logit_scale,
    conv_gain,
    glu_proj,
    kernel,
    post_gain,
    mix_proj,
    cotangent,
):
    head_count = lax.axis_size("head")
    shard_count = lax.axis_size("tm")
    head_place = lax.axis_index("head")
    shard_place = lax.axis_index("tm")
    local_frames, width = frames.shape
    conv_rows = local_frames // head_count
    local_width = qkv_proj.shape[2]
    all_frames = local_frames * shard_count
    devices = head_count * shard_count
    ends = jnp.cumsum(segment_lengths).astype(jnp.int32)

    def segment_of(positions):
        located = jnp.sum((ends[None, :] <= positions[:, None]).astype(jnp.int32), axis=1)
        return jnp.where(positions < 0, -1, located)

    bits = []
    bit = shard_count // 2
    while bit:
        bits.append(bit)
        bit //= 2
    other_bits = bits[-2:-1] + bits[:-2] + bits[-1:]
    ids = slot_order(bits)
    alternate = slot_order(other_bits)
    places = ((head_place - jnp.arange(head_count)) % head_count).astype(jnp.int32)

    halo = MOST + PAD
    even = shard_place % 2 == 0
    near = flip(jnp.where(even, frames[-halo:], frames[:halo]), 1)
    away = jnp.where(even, frames[:halo], frames[-halo:])
    halves = 2 if head_count == 2 else 1
    share_rows = halo // halves
    if halves == 2:
        away = lax.dynamic_slice_in_dim(away, head_place * share_rows, share_rows, 0)
    mine = lax.ppermute(away, "tm", tm_pairs())

    key_cells, value_cells, query_cells = qkv_proj[:, 1], qkv_proj[:, 2], qkv_proj[:, 0]
    key_steps, value_steps, query_steps = [key_cells], [value_cells], [query_cells]
    for level in range(len(bits) - 1):
        key_steps.append(grow(key_steps[-1], bits[level]))
        value_steps.append(grow(value_steps[-1], bits[level]))
        query_steps.append(grow(query_steps[-1], other_bits[level]))
    key_halves = (key_steps[-1], flip(key_steps[-1], bits[-1]))
    value_halves = (value_steps[-1], flip(value_steps[-1], bits[-1]))
    query_halves = (query_steps[-1], flip(query_steps[-1], bits[-1]))
    one_shard = jnp.concatenate([out_proj.T, glu_proj[:, :width]], axis=1)
    two_shard = jnp.concatenate([glu_proj[:, width:], mix_proj], axis=1)
    one_cells = grow(one_shard, bits[0], key_steps[2])
    two_cells = grow(two_shard, other_bits[0], key_steps[2])

    away_place = jnp.where(even, 0, halo + local_frames)
    pieces = [frames, near, mine]
    piece_places = [halo, halo + local_frames - away_place, away_place]
    if halves == 2:
        pieces.append(lax.ppermute(mine, "head", [(0, 1), (1, 0)]))
        piece_places[2] = away_place + head_place * share_rows
        piece_places.append(away_place + (1 - head_place) * share_rows)
    piece_places = jnp.stack([jnp.asarray(p, jnp.int32) for p in piece_places])
    normed = norm_rows(piece_places, attn_gain[None, :], pieces)
    key_rows = local_frames + 2 * halo
    scale = jnp.repeat(logit_scale * (math.log2(math.e) / HD), HD)[None, :]
    keys, values, queries = project(
        ids, alternate, normed, key_halves, value_halves, query_halves, scale
    )
    query_rows = local_frames + 2 * PAD

    for level in range(1, len(bits) - 1):
        reason = queries if level == len(bits) - 2 else normed
        one_cells = grow(one_cells, bits[level], reason)
        two_cells = grow(two_cells, other_bits[level], reason)

    conv_all = conv_rows + 2 * RIM
    def beside(block, near, away):
        before = jnp.where(even, away, near)
        return jnp.concatenate([before, block, jnp.where(even, near, away)], axis=0)

    cotangent_all = beside(
        cotangent,
        flip(after(jnp.where(even, cotangent[-RIM:], cotangent[:RIM]), key_steps[2]), 1),
        lax.ppermute(
            after(jnp.where(even, cotangent[:RIM], cotangent[-RIM:]), key_steps[2]),
            "tm",
            tm_pairs(),
        ),
    )
    conv_window = lambda rows, d: lax.dynamic_slice_in_dim(rows, d * conv_rows, conv_all, 0)
    upstream = jnp.stack(
        to_heads(functools.partial(conv_window, after(cotangent_all, normed))), 0
    )

    base = shard_place * local_frames
    key_positions = base - halo + jnp.arange(key_rows, dtype=jnp.int32)
    key_segment = segment_of(key_positions)
    query_segment = key_segment[MOST : MOST + query_rows]
    block = math.gcd(query_rows, 3 * LANE)
    query_blocks = query_rows // block
    first_frame = base - PAD + block * jnp.arange(query_blocks, dtype=jnp.int32)
    last_frame = first_frame + block - 1
    low = jnp.max(jnp.where(ends[None, :] <= first_frame[:, None], ends[None, :], 0), axis=1)
    low = jnp.where(first_frame < 0, base - halo, low)
    high = jnp.min(
        jnp.where(ends[None, :] > last_frame[:, None], ends[None, :], 2 * all_frames), axis=1
    )
    low = jnp.clip(low - (base - halo), 0, key_rows - KEYS)
    high = jnp.clip(high - (base - halo), 0, key_rows)
    start = (low // LANE) * LANE
    count = jnp.maximum((high - start + KEYS - 1) // KEYS, 1)
    start = jnp.maximum(jnp.minimum(start, key_rows - KEYS * count), 0)
    count = jnp.minimum(count, key_rows // KEYS)
    heads_out = attend(
        start, count, queries[MOST : MOST + query_rows], keys, values, query_segment[:, None], key_segment[None, :]
    )

    window = lambda d: lax.dynamic_slice_in_dim(
        heads_out, PAD - RIM + d * conv_rows, conv_all, 0
    )
    heads_out = after(heads_out, upstream)
    heads_all = jnp.stack(to_heads(window), 0)
    one_halves = (one_cells, flip(after(one_cells, heads_out), bits[-1]))
    two_halves = (two_cells, flip(after(two_cells, heads_out), bits[-1]))

    if halves == 2:
        first_half = jnp.where(head_place == 0, pieces[2][:RIM], pieces[3][:RIM])
        last_half = jnp.where(head_place == 0, pieces[3][-RIM:], pieces[2][-RIM:])
    else:
        first_half, last_half = mine[:RIM], mine[-RIM:]
    frame_rows = conv_window(
        beside(
            frames,
            jnp.where(even, near[:RIM], near[-RIM:]),
            jnp.where(even, last_half, first_half),
        ),
        head_place,
    )
    conv_first = base + head_place * conv_rows - RIM
    limits = jnp.concatenate([jnp.zeros((1,), jnp.int32), ends])
    limits = jnp.concatenate(
        [
            jnp.clip(limits - conv_first, 0, conv_all),
            jnp.sum((ends <= conv_first).astype(jnp.int32), keepdims=True),
            jnp.sum((limits[:-1] < conv_first + conv_all).astype(jnp.int32), keepdims=True),
        ]
    )
    taps = kernel.reshape(KERNEL * (width // LANE), LANE)

    residual, gated, value, gate = open_block(
        ids, alternate, places, heads_all, frame_rows, conv_gain[None, :], one_halves, two_halves
    )
    *out_parts, depth_grad, post_sum = middle_block(
        alternate, places, limits, upstream, gated, residual, taps, post_gain[None, :], two_halves
    )
    out_frames = in_order(send_heads(out_parts))
    glu_grad, taps_sum = spread_block(limits, depth_grad, gated, value, gate, taps)
    tap_rows = taps_sum.reshape(KERNEL, width)
    first_terms = jnp.concatenate([tap_rows, jnp.sum(post_sum, axis=0, keepdims=True)], axis=0)
    scattered = lax.all_to_all(
        first_terms.reshape(devices, (KERNEL + 1) * width // devices),
        ("head", "tm"),
        split_axis=0,
        concat_axis=0,
        tiled=True,
    )
    share = jnp.sum(scattered, axis=0)
    *grad_parts, open_sum = close_block(
        ids,
        alternate,
        places,
        upstream,
        after(glu_grad, out_frames),
        residual,
        conv_gain[None, :],
        one_halves,
        two_halves,
    )
    grad_input = in_order(send_heads(grad_parts))
    last_terms = jnp.concatenate([share, jnp.sum(open_sum, axis=0)], axis=0)
    everywhere = lax.all_to_all(
        jnp.broadcast_to(last_terms[None], (devices, last_terms.shape[0])),
        ("head", "tm"),
        split_axis=0,
        concat_axis=0,
        tiled=True,
    )
    grad_scale = 1.0 / math.sqrt(all_frames)
    reduced = everywhere[:, : share.shape[0]].reshape(KERNEL + 1, width)
    open_total = jnp.sum(everywhere[:, share.shape[0] :], axis=0)
    gains = jnp.stack([open_total, reduced[KERNEL]], axis=0)
    return (out_frames, grad_input, reduced[:KERNEL] * grad_scale, gains * grad_scale)


def solution(mesh):
    placed = (
        P("tm", None),
        P(),
        P(),
        P("tm", None, "head"),
        P(None, "tm"),
        P("head"),
        P(),
        P("tm", None),
        P(),
        P(),
        P("tm", None),
        P("tm", "head"),
    )
    return jax.shard_map(
        on_device,
        mesh=mesh,
        in_specs=placed,
        out_specs=(P("tm", "head"), P("tm", "head"), P(), P()),
        check_vma=False,
    )
```

```python
import functools
import math

import jax
import jax.numpy as jnp
from jax import lax
from jax.experimental import pallas as pl
from jax.experimental.pallas import tpu as pltpu
from jax.sharding import PartitionSpec as P

HD = 64
KERNEL = 31
HALF = 15
MOST = 512
LANE = 128
RIM = 32
EDGE = 16
KEYS = 256

EPS_NORM = 1e-05
EPS_HEAD = 1e-06


F32 = jnp.float32
BF16 = jnp.bfloat16
VMEM_SPEC = pl.BlockSpec(memory_space=pltpu.VMEM)
ANY_SPEC = pl.BlockSpec(memory_space=pltpu.HBM)
SMEM_SPEC = pl.BlockSpec(memory_space=pltpu.SMEM)


def tile_of(count, most):
    best = 16
    for size in range(16, most + 1, 16):
        if count % size == 0:
            best = size
    return best


def dot_nn(a, b):
    return lax.dot_general(a, b, (((1,), (0,)), ((), ())), preferred_element_type=F32)


def dot_nt(a, b):
    return lax.dot_general(a, b, (((1,), (1,)), ((), ())), preferred_element_type=F32)


def row_stats(values):
    average = jnp.mean(values, axis=-1, keepdims=True)
    centred = values - average
    inverse = lax.rsqrt(jnp.mean(centred * centred, axis=-1, keepdims=True) + EPS_NORM)
    return centred * inverse, inverse


def slot_copies(ids_ref, halves, target, sems, column=0):
    slots = ids_ref.shape[0]
    each = slots // len(halves)
    rows = target.shape[0] // slots
    columns = pl.ds(column, target.shape[1])
    copies = []
    for slot in range(slots):
        source = halves[slot // each].at[pl.ds((slot % each) * rows, rows), columns]
        place = pl.multiple_of(ids_ref[slot] * rows, rows)
        copies.append(
            pltpu.make_async_copy(source, target.at[pl.ds(place, rows), :], sems.at[slot])
        )
    return copies


def start_all(copies):
    for copy in copies:
        copy.start()


def wait_all(copies):
    for copy in copies:
        copy.wait()


def cost(flops, moved):
    return pl.CostEstimate(flops=flops, transcendentals=0, bytes_accessed=moved)


def norm_kernel(x_ref, gain_ref, out_ref):
    normed, _ = row_stats(x_ref[...].astype(F32))
    out_ref[...] = (normed * gain_ref[...]).astype(BF16)


def norm_rows(x, gain):
    rows, width = x.shape
    tile = tile_of(rows, 256)
    return pl.pallas_call(
        norm_kernel,
        grid=(rows // tile,),
        in_specs=[
            pl.BlockSpec((tile, width), lambda i: (i, 0)),
            pl.BlockSpec((1, width), lambda i: (0, 0)),
        ],
        out_specs=pl.BlockSpec((tile, width), lambda i: (i, 0)),
        out_shape=jax.ShapeDtypeStruct((rows, width), BF16),
        cost_estimate=cost(0, 12 * rows * width),
        name="norm_rows",
    )(x, gain)


def qkv_kernel(pieces, ids_ref, alt_ref, even_ref, x_ref, scale_ref, *refs):
    kv_refs, q_refs, refs = refs[:pieces], refs[pieces : 2 * pieces], refs[2 * pieces :]
    kv_out, q_out, near_out, away_out = refs[:4]
    k_weight, v_weight, q_weight, k_sems, v_sems, q_sems = refs[4:]
    first = pl.program_id(0) == 0
    k_copies = slot_copies(ids_ref, kv_refs, k_weight, k_sems)
    v_copies = slot_copies(
        ids_ref, kv_refs, v_weight, v_sems, k_weight.shape[1]
    )
    q_copies = slot_copies(alt_ref, q_refs, q_weight, q_sems)

    @pl.when(first)
    def _():
        start_all(k_copies + v_copies + q_copies)
        wait_all(k_copies)

    x = x_ref[...]
    width = k_weight.shape[1]
    group = min(KEYS, width)
    row_head = lax.broadcasted_iota(jnp.int32, (group, group), 0) // HD
    column_head = lax.broadcasted_iota(jnp.int32, (group, group), 1) // HD
    ones = jnp.where(row_head == column_head, 1.0, 0.0).astype(BF16)

    def unit(product, out, scale):
        for start in range(0, width, group):
            part = product[:, start : start + group]
            total = dot_nn((part * part).astype(BF16), ones)
            scaled = part * lax.rsqrt(total * (1.0 / HD) + EPS_HEAD)
            if scale is not None:
                scaled = scaled * scale[:, start : start + group]
            out[:, start : start + group] = scaled.astype(BF16)

    unit(dot_nn(x, k_weight[...]), kv_out, None)

    @pl.when(first)
    def _():
        wait_all(v_copies)

    kv_out[:, width:] = dot_nn(x, v_weight[...]).astype(BF16)

    @pl.when(first)
    def _():
        wait_all(q_copies)

    step, last = pl.program_id(0), pl.num_programs(0) - 1
    is_even = even_ref[0] == 1

    @pl.when(((step == last) & is_even) | ((step == 0) & jnp.logical_not(is_even)))
    def _():
        near_out[...] = kv_out[...]

    @pl.when(((step == 0) & is_even) | ((step == last) & jnp.logical_not(is_even)))
    def _():
        away_out[...] = kv_out[...]

    unit(dot_nn(x, q_weight[...]), q_out, scale_ref)


def project(ids, alternate, even, x, key_value_pieces, query_pieces, scale):
    rows, width = x.shape
    columns = query_pieces[0].shape[1]
    slots = ids.shape[0]
    tile = MOST
    pieces = len(query_pieces)
    return pl.pallas_call(
        functools.partial(qkv_kernel, pieces),
        grid_spec=pltpu.PrefetchScalarGridSpec(
            num_scalar_prefetch=3,
            grid=(rows // tile,),
            in_specs=[
                pl.BlockSpec((tile, width), lambda i, a, b, c: (i, 0)),
                pl.BlockSpec((1, columns), lambda i, a, b, c: (0, 0)),
            ]
            + [ANY_SPEC] * (2 * pieces),
            out_specs=[
                pl.BlockSpec((tile, 2 * columns), lambda i, a, b, c: (i, 0)),
                pl.BlockSpec((tile, columns), lambda i, a, b, c: (i, 0)),
                pl.BlockSpec((tile, 2 * columns), lambda i, a, b, c: (0, 0)),
                pl.BlockSpec((tile, 2 * columns), lambda i, a, b, c: (0, 0)),
            ],
            scratch_shapes=[pltpu.VMEM((width, columns), BF16)] * 3
            + [pltpu.SemaphoreType.DMA((slots,))] * 3,
        ),
        out_shape=[
            jax.ShapeDtypeStruct((rows, 2 * columns), BF16),
            jax.ShapeDtypeStruct((rows, columns), BF16),
            jax.ShapeDtypeStruct((tile, 2 * columns), BF16),
            jax.ShapeDtypeStruct((tile, 2 * columns), BF16),
        ],
        cost_estimate=cost(6 * rows * width * columns, 12 * width * width),
        name="project",
    )(ids, alternate, even, x, scale, *key_value_pieces, *query_pieces)


def attend_step(acc, q_ref, kv_ref, qseg_ref, kseg_ref, bias_ref, start):
    rows, width = q_ref.shape
    lane = lax.broadcasted_iota(jnp.int32, (rows, LANE), 1)
    lane_keys = lax.broadcasted_iota(jnp.int32, (KEYS, LANE), 1)
    same = qseg_ref[...] == kseg_ref[:, pl.ds(start, KEYS)]
    bias_ref[...] = jnp.where(same, 0.0, -1e30)
    for pair in range(width // LANE):
        queries = q_ref[:, pl.ds(pair * LANE, LANE)]
        keys = kv_ref[pl.ds(start, KEYS), pl.ds(pair * LANE, LANE)]
        values = kv_ref[pl.ds(start, KEYS), pl.ds(width + pair * LANE, LANE)]
        for side in range(2):
            mine = (lane < HD) if side == 0 else (lane >= HD)
            mine_keys = (lane_keys < HD) if side == 0 else (lane_keys >= HD)
            one = jnp.where(mine, queries, jnp.zeros_like(queries))
            scores = dot_nt(one, keys) + bias_ref[...]
            weights = jnp.exp2(scores).astype(BF16)
            extended = jnp.where(mine_keys, values, jnp.ones_like(values))
            acc[2 * pair + side] += dot_nn(weights, extended)


def attend_own_kernel(first_ref, count_ref, q_ref, kv_ref, qseg_ref, kseg_ref, acc_ref, bias_ref):
    block = pl.program_id(0)
    acc_ref[...] = jnp.zeros_like(acc_ref)

    def step(index, carry):
        start = pl.multiple_of(first_ref[block] + index * KEYS, LANE)
        attend_step(acc_ref, q_ref, kv_ref, qseg_ref, kseg_ref, bias_ref, start)
        return carry

    lax.fori_loop(0, count_ref[block], step, 0)


def attend_rest_kernel(
    first_ref, count_ref, even_ref, q_ref, near_ref, away_ref, qseg_ref, kseg_ref, own_ref,
    out_ref, acc_ref, bias_ref, kv_ref, sems,
):
    half = near_ref.shape[0]
    near_place = pl.multiple_of(even_ref[0] * half, half)
    away_place = pl.multiple_of((1 - even_ref[0]) * half, half)

    @pl.when(pl.program_id(0) == 0)
    def _():
        copies = [
            pltpu.make_async_copy(near_ref, kv_ref.at[pl.ds(near_place, half), :], sems.at[0]),
            pltpu.make_async_copy(away_ref, kv_ref.at[pl.ds(away_place, half), :], sems.at[1]),
        ]
        start_all(copies)
        wait_all(copies)

    block = pl.program_id(0)
    rows, width = q_ref.shape
    lane = lax.broadcasted_iota(jnp.int32, (rows, LANE), 1)

    def finish(acc):
        for pair in range(width // LANE):
            even, odd = acc[2 * pair], acc[2 * pair + 1]
            above = jnp.where(lane < HD, even, odd)
            below = pltpu.roll(jnp.where(lane < HD, odd, even), HD, 1)
            out_ref[:, pl.ds(pair * LANE, LANE)] = (above / below).astype(BF16)

    def step(index, carry):
        start = pl.multiple_of(first_ref[block] + index * KEYS, LANE)
        attend_step(acc_ref, q_ref, kv_ref, qseg_ref, kseg_ref, bias_ref, start)
        return carry

    @pl.when(count_ref[block] == 0)
    def _():
        finish(own_ref)

    @pl.when(count_ref[block] > 0)
    def _():
        acc_ref[...] = own_ref[...]
        lax.fori_loop(0, count_ref[block], step, 0)
        finish(acc_ref)


def attend_own(first, count, queries, key_value, segment):
    rows, width = queries.shape
    block = rows // first.shape[0]
    heads = width // HD
    return pl.pallas_call(
        attend_own_kernel,
        grid_spec=pltpu.PrefetchScalarGridSpec(
            num_scalar_prefetch=2,
            grid=(rows // block,),
            in_specs=[
                pl.BlockSpec((block, width), lambda i, a, b: (i, 0)),
                pl.BlockSpec((rows, 2 * width), lambda i, a, b: (0, 0)),
                pl.BlockSpec((block, 1), lambda i, a, b: (i, 0)),
                pl.BlockSpec((1, rows), lambda i, a, b: (0, 0)),
            ],
            out_specs=pl.BlockSpec((heads, block, LANE), lambda i, a, b: (0, i, 0)),
            scratch_shapes=[pltpu.VMEM((block, KEYS), F32)],
        ),
        out_shape=jax.ShapeDtypeStruct((heads, rows, LANE), F32),
        cost_estimate=cost(16 * rows * width * width, 20 * rows * width),
        name="attend_own",
    )(first, count, queries, key_value, segment[:, None], segment[None, :])


def attend_rest(first, count, even, queries, near, away, segment, key_segment, own):
    rows, width = queries.shape
    block = rows // first.shape[0]
    heads = width // HD
    keys = 2 * near.shape[0]
    return pl.pallas_call(
        attend_rest_kernel,
        grid_spec=pltpu.PrefetchScalarGridSpec(
            num_scalar_prefetch=3,
            grid=(rows // block,),
            in_specs=[
                pl.BlockSpec((block, width), lambda i, a, b, c: (i, 0)),
                ANY_SPEC,
                ANY_SPEC,
                pl.BlockSpec((block, 1), lambda i, a, b, c: (i, 0)),
                pl.BlockSpec((1, keys), lambda i, a, b, c: (0, 0)),
                pl.BlockSpec((heads, block, LANE), lambda i, a, b, c: (0, i, 0)),
            ],
            out_specs=pl.BlockSpec((block, width), lambda i, a, b, c: (i, 0)),
            scratch_shapes=[
                pltpu.VMEM((heads, block, LANE), F32),
                pltpu.VMEM((block, KEYS), F32),
                pltpu.VMEM((keys, 2 * width), BF16),
                pltpu.SemaphoreType.DMA((2,)),
            ],
        ),
        out_shape=jax.ShapeDtypeStruct((rows, width), BF16),
        cost_estimate=cost(4 * rows * width * width, 20 * rows * width),
        name="attend_rest",
    )(first, count, even, queries, near, away, segment[:, None], key_segment[None, :], own)


def open_kernel(
    parts, slabs, ids_ref, alt_ref, place_ref, *refs
):
    heads_refs = refs[:parts]
    (frames_ref, gain_ref) = refs[parts : parts + 2]
    refs = refs[parts + 2 :]
    ones, twos, refs = refs[:slabs], refs[slabs : 2 * slabs], refs[2 * slabs :]
    (res_ref, gated_ref, value_ref, gate_ref) = refs[:4]
    out_weight, value_weight, gate_weight, out_sems, value_sems, gate_sems = refs[4:]

    width = frames_ref.shape[1]
    first = pl.program_id(0) == 0
    out_copies = slot_copies(ids_ref, ones, out_weight, out_sems)
    glu_copies = slot_copies(ids_ref, ones, value_weight, value_sems, width)
    glu_copies += slot_copies(alt_ref, twos, gate_weight, gate_sems)

    @pl.when(first)
    def _():
        start_all(out_copies + glu_copies)
        wait_all(out_copies)

    heads = jnp.concatenate([ref[0] for ref in heads_refs], axis=1)
    total = frames_ref[...].astype(F32) + dot_nt(heads, out_weight[...])
    residual = total.astype(BF16)
    res_ref[...] = residual
    normed, _ = row_stats(residual.astype(F32))
    conv_input = (normed * gain_ref[...]).astype(BF16)

    @pl.when(first)
    def _():
        wait_all(glu_copies)

    value = dot_nn(conv_input, value_weight[...])
    gate = jax.nn.sigmoid(dot_nn(conv_input, gate_weight[...]))
    value_ref[...] = value
    gate_ref[...] = gate
    gated_ref[...] = (value * gate).astype(BF16)


def open_block(ids, alternate, places, heads, frames, gain, one_halves, two_halves):
    parts, rows, local = heads.shape
    width = frames.shape[1]
    tile = tile_of(rows, 288)
    slots = ids.shape[0]

    def head_spec(source):
        return pl.BlockSpec((1, tile, local), lambda i, a, b, place: (place[source], i, 0))

    row_spec = pl.BlockSpec((tile, width), lambda i, a, b, place: (i, 0))
    return pl.pallas_call(
        functools.partial(open_kernel, parts, len(one_halves)),
        grid_spec=pltpu.PrefetchScalarGridSpec(
            num_scalar_prefetch=3,
            grid=(rows // tile,),
            in_specs=[head_spec(s) for s in range(parts)]
            + [row_spec, pl.BlockSpec((1, width), lambda i, a, b, place: (0, 0))]
            + [ANY_SPEC] * (2 * len(one_halves)),
            out_specs=[row_spec] * 4,
            scratch_shapes=[
                pltpu.VMEM((width, width), BF16),
                pltpu.VMEM((width, width), BF16),
                pltpu.VMEM((width, width), BF16),
                pltpu.SemaphoreType.DMA((slots,)),
                pltpu.SemaphoreType.DMA((slots,)),
                pltpu.SemaphoreType.DMA((slots,)),
            ],
        ),
        out_shape=[
            jax.ShapeDtypeStruct((rows, width), BF16),
            jax.ShapeDtypeStruct((rows, width), BF16),
            jax.ShapeDtypeStruct((rows, width), F32),
            jax.ShapeDtypeStruct((rows, width), F32),
        ],
        cost_estimate=cost(10 * rows * width * width, 24 * rows * width),
        name="open_block",
    )(ids, alternate, places, *([heads] * parts), frames, gain, *one_halves, *two_halves)


SUB = 8
STEP = 8
SPAN = STEP + KERNEL - 1
LEAD = 16


def at_frame(frame, frames=1, tile=SUB):
    start = frame * tile
    if not isinstance(start, int):
        start = pl.multiple_of(start, SUB)
    return pl.ds(start, frames * tile)


def to_frames(source_ref, target, count, shift):
    width = source_ref.shape[1]
    tile = width // LANE

    def step(index, carry):
        start = pl.multiple_of(index * 16, 16)
        for block in range(tile):
            values = source_ref[pl.ds(start, 16), block * LANE : (block + 1) * LANE].astype(F32)
            target[pl.ds((start + shift) * tile + block, 16, stride=tile), :] = values
        return carry

    lax.fori_loop(0, count // 16, step, 0)


def copy_frames(source, target, first, place, count, tile):
    def step(index, carry):
        source_at = at_frame(first + index * STEP, STEP, tile)
        target[at_frame(place + index * STEP, STEP, tile), :] = source[source_at, :]
        return carry

    lax.fori_loop(0, (count + STEP - 1) // STEP, step, 0)


def deal(rows_ref, out_refs, place_ref, start):
    parts = len(out_refs)
    rows, width = rows_ref.shape
    local = width // parts
    for shift, out_ref in enumerate(out_refs):
        head = lax.rem(place_ref[0] + shift, parts)
        columns = pl.ds(pl.multiple_of(head * local, local), local)
        out_ref[pl.ds(start, rows), :] = rows_ref[:, columns]


def middle_kernel(parts, slabs, ids_ref, place_ref, limits_ref, *refs):
    up_refs = refs[:parts]
    (gated_ref, res_ref, taps_ref, gain_ref) = refs[parts : parts + 4]
    refs = refs[parts + 4 :]
    twos, out_refs, refs = refs[:slabs], refs[slabs : slabs + parts], refs[slabs + parts :]
    (grad_ref, gain_out, cells, buffer, depth, back, swished, mix, turned, sems) = refs
    rows, width = gated_ref.shape
    blocks = width // LANE
    inner = rows - 2 * EDGE
    own = rows - 2 * RIM

    copies = slot_copies(ids_ref, twos, mix, sems, width)
    start_all(copies)

    depth[...] = jnp.zeros_like(depth)
    buffer[at_frame(0, LEAD, blocks), :] = jnp.zeros((LEAD * blocks, LANE), F32)
    to_frames(gated_ref, cells, rows, 0)
    segments = limits_ref.shape[0] - 3

    def segment_step(segment, carry):
        first, last = limits_ref[segment], limits_ref[segment + 1]
        length = last - first
        copy_frames(cells, buffer, first, LEAD, length, blocks)
        zeros = jnp.zeros(((LEAD + STEP) * blocks, LANE), F32)
        buffer[at_frame(LEAD + length, LEAD + STEP, blocks), :] = zeros

        def convolve(index, carry):
            start = index * STEP
            sums = [None] * STEP
            for near in range(SPAN):
                frame = buffer[at_frame(start + LEAD - HALF + near, 1, blocks), :]
                for one in range(STEP):
                    tap = near - one
                    if 0 <= tap < KERNEL:
                        term = taps_ref[tap * blocks : (tap + 1) * blocks, :] * frame
                        sums[one] = term if sums[one] is None else sums[one] + term
            for one in range(STEP):
                depth[at_frame(first + start + one, 1, blocks), :] = sums[one]
            return carry

        lax.fori_loop(0, (length + STEP - 1) // STEP, convolve, 0)
        return carry

    lax.fori_loop(limits_ref[segments + 1], limits_ref[segments + 2], segment_step, 0)

    wait_all(copies)

    big = tile_of(inner, 288)

    def backward(index, carry):
        start = pl.multiple_of(index * big, 16)
        upstream = jnp.concatenate(
            [ref[0, pl.ds(start + EDGE, big), :] for ref in up_refs], axis=1
        )
        back[pl.ds(start, big), :] = dot_nt(upstream, mix[...])
        return carry

    lax.fori_loop(0, inner // big, backward, 0)
    gain_out[...] = jnp.zeros_like(gain_out)

    def pointwise(index, carry):
        start = pl.multiple_of(index * 16, 16)
        cuts = [slice(b * LANE, (b + 1) * LANE) for b in range(blocks)]
        values = [
            depth[pl.ds((start + EDGE) * blocks + b, 16, stride=blocks), :] for b in range(blocks)
        ]
        average = jnp.sum(functools.reduce(jnp.add, values), axis=1, keepdims=True) / width
        values = [v - average for v in values]
        spread_of = (
            jnp.sum(functools.reduce(jnp.add, [v * v for v in values]), axis=1, keepdims=True)
            / width
        )
        inverse = lax.rsqrt(spread_of + EPS_NORM)
        scaled, first_sum, second_sum = [], 0.0, 0.0
        is_own = jnp.where((index >= 1) & (index < 1 + own // 16), 1.0, 0.0)
        for b in range(blocks):
            normed = values[b] * inverse
            post = normed * gain_ref[:, cuts[b]]
            gate = jax.nn.sigmoid(post)
            swished[pl.ds(start, 16), cuts[b]] = (post * gate).astype(BF16)
            grad = back[pl.ds(start, 16), cuts[b]] * (gate * (1.0 + post * (1.0 - gate)))
            term = grad * normed
            gain_out[:, cuts[b]] += (term[:8] + term[8:]) * is_own
            part = grad * gain_ref[:, cuts[b]]
            scaled.append(part)
            first_sum = first_sum + part
            second_sum = second_sum + part * normed
            values[b] = normed
        first_mean = jnp.sum(first_sum, axis=1, keepdims=True) / width
        second_mean = jnp.sum(second_sum, axis=1, keepdims=True) / width
        for b in range(blocks):
            grad_ref[pl.ds(start, 16), cuts[b]] = (
                inverse * (scaled[b] - first_mean - values[b] * second_mean)
            ).astype(BF16)
        return carry

    lax.fori_loop(0, inner // 16, pointwise, 0)

    big = tile_of(own, 256)

    def forward(index, carry):
        start = pl.multiple_of(index * big, 16)
        product = dot_nn(swished[pl.ds(start + EDGE, big), :], mix[...])
        turned[...] = (res_ref[pl.ds(start + RIM, big), :].astype(F32) + product).astype(BF16)
        deal(turned, out_refs, place_ref, start)
        return carry

    lax.fori_loop(0, own // big, forward, 0)


def middle_block(ids, places, limits, upstream, gated, residual, taps, gain, mix_halves):
    parts, rows, local = upstream.shape
    width = gated.shape[1]
    slots = ids.shape[0]
    inner, own = rows - 2 * EDGE, rows - 2 * RIM
    blocks = width // LANE

    def up_spec(source):
        return pl.BlockSpec((1, rows, local), lambda i, a, place, b: (place[source], 0, 0))

    return pl.pallas_call(
        functools.partial(middle_kernel, parts, len(mix_halves)),
        grid_spec=pltpu.PrefetchScalarGridSpec(
            num_scalar_prefetch=3,
            grid=(1,),
            in_specs=[up_spec(s) for s in range(parts)] + [VMEM_SPEC] * 4
            + [ANY_SPEC] * len(mix_halves),
            out_specs=[VMEM_SPEC] * (parts + 2),
            scratch_shapes=[
                pltpu.VMEM(((rows + STEP) * blocks, LANE), F32),
                pltpu.VMEM(((rows + 2 * LEAD + STEP) * blocks, LANE), F32),
                pltpu.VMEM(((rows + STEP) * blocks, LANE), F32),
                pltpu.VMEM((inner, width), F32),
                pltpu.VMEM((inner, width), BF16),
                pltpu.VMEM((width, width), BF16),
                pltpu.VMEM((tile_of(own, 256), width), BF16),
                pltpu.SemaphoreType.DMA((slots,)),
            ],
        ),
        out_shape=[jax.ShapeDtypeStruct((own, width // parts), BF16)] * parts
        + [
            jax.ShapeDtypeStruct((inner, width), BF16),
            jax.ShapeDtypeStruct((8, width), F32),
        ],
        cost_estimate=cost(4 * rows * width * width, 60 * rows * width),
        name="middle_block",
    )(ids, places, limits, *([upstream] * parts), gated, residual, taps, gain, *mix_halves)


def spread_kernel(
    limits_ref, grad_ref, gated_ref, value_ref, gate_ref, taps_ref, out_ref, taps_out,
    cells, inputs, buffer, held, total,
):
    rows, width = gated_ref.shape
    blocks = width // LANE
    inner, own = rows - 2 * EDGE, rows - 2 * RIM
    taps_out[...] = jnp.zeros_like(taps_out)
    total[...] = jnp.zeros_like(total)
    buffer[at_frame(0, LEAD, blocks), :] = jnp.zeros((LEAD * blocks, LANE), F32)
    to_frames(grad_ref, cells, inner, EDGE)
    to_frames(gated_ref, inputs, rows, 0)
    segments = limits_ref.shape[0] - 3

    def segment_step(segment, carry):
        first, last = limits_ref[segment], limits_ref[segment + 1]
        own_first, own_last = jnp.maximum(first, RIM), jnp.minimum(last, rows - RIM)
        first, last = jnp.maximum(first, EDGE), jnp.minimum(last, rows - EDGE)

        @pl.when(own_last > own_first)
        def _():
            length, own_length = last - first, own_last - own_first
            skip = own_first - first
            copy_frames(cells, buffer, first, LEAD, length, blocks)
            zeros = jnp.zeros(((LEAD + STEP) * blocks, LANE), F32)
            buffer[at_frame(LEAD + length, LEAD + STEP, blocks), :] = zeros
            copy_frames(inputs, held, own_first, 0, own_length, blocks)
            held[at_frame(own_length, STEP, blocks), :] = jnp.zeros((STEP * blocks, LANE), F32)

            def convolve(index, carry):
                start = index * STEP
                sums = [None] * STEP
                mine = [held[at_frame(start + one, 1, blocks), :] for one in range(STEP)]
                terms = [None] * KERNEL
                for near in range(SPAN):
                    frame = buffer[at_frame(start + skip + LEAD - HALF + near, 1, blocks), :]
                    for one in range(STEP):
                        tap = one + KERNEL - 1 - near
                        if 0 <= tap < KERNEL:
                            place = slice(tap * blocks, (tap + 1) * blocks)
                            term = taps_ref[place, :] * frame
                            sums[one] = term if sums[one] is None else sums[one] + term
                            term = mine[one] * frame
                            terms[tap] = term if terms[tap] is None else terms[tap] + term
                    done = KERNEL - 1 + STEP - 1 - near
                    if 0 <= done < KERNEL:
                        taps_out[done * blocks : (done + 1) * blocks, :] += terms[done]
                for one in range(STEP):
                    total[at_frame(own_first + start + one, 1, blocks), :] = sums[one]
                return carry

            lax.fori_loop(0, (own_length + STEP - 1) // STEP, convolve, 0)

        return carry

    lax.fori_loop(limits_ref[segments + 1], limits_ref[segments + 2], segment_step, 0)

    def gates(index, carry):
        start = pl.multiple_of(index * 16, 16)
        for block in range(blocks):
            columns = slice(block * LANE, (block + 1) * LANE)
            gate = gate_ref[pl.ds(start + RIM, 16), columns]
            value = value_ref[pl.ds(start + RIM, 16), columns]
            through = total[pl.ds((start + RIM) * blocks + block, 16, stride=blocks), :] * gate
            out_ref[pl.ds(start, 16), columns] = through.astype(BF16)
            out_ref[pl.ds(start, 16), width + block * LANE : width + (block + 1) * LANE] = (
                through * value * (1.0 - gate)
            ).astype(BF16)
        return carry

    lax.fori_loop(0, own // 16, gates, 0)


def spread_block(limits, grad, gated, value, gate, taps):
    rows, width = gated.shape
    inner, own = rows - 2 * EDGE, rows - 2 * RIM
    blocks = width // LANE
    return pl.pallas_call(
        spread_kernel,
        grid_spec=pltpu.PrefetchScalarGridSpec(
            num_scalar_prefetch=1,
            grid=(1,),
            in_specs=[VMEM_SPEC] * 5,
            out_specs=[VMEM_SPEC] * 2,
            scratch_shapes=[
                pltpu.VMEM(((rows + STEP) * blocks, LANE), F32),
                pltpu.VMEM(((rows + STEP) * blocks, LANE), F32),
                pltpu.VMEM(((rows + 2 * LEAD + STEP) * blocks, LANE), F32),
                pltpu.VMEM(((own + 2 * STEP) * blocks, LANE), F32),
                pltpu.VMEM(((rows + STEP) * blocks, LANE), F32),
            ],
        ),
        out_shape=[
            jax.ShapeDtypeStruct((own, 2 * width), BF16),
            jax.ShapeDtypeStruct((KERNEL * blocks, LANE), F32),
        ],
        cost_estimate=cost(0, 70 * own * width),
        name="spread_block",
    )(limits, grad, gated, value, gate, taps)


def close_kernel(parts, slabs, ids_ref, alt_ref, place_ref, *refs):
    up_refs = refs[:parts]
    (grad_ref, res_ref, gain_ref) = refs[parts : parts + 3]
    refs = refs[parts + 3 :]
    ones, twos, refs = refs[:slabs], refs[slabs : 2 * slabs], refs[2 * slabs :]
    out_refs, gain_out = refs[:parts], refs[parts]
    (value_weight, gate_weight, turned, value_sems, gate_sems) = refs[parts + 1 :]
    own, width = grad_ref.shape[0], res_ref.shape[1]
    copies = slot_copies(ids_ref, ones, value_weight, value_sems, width)
    copies += slot_copies(alt_ref, twos, gate_weight, gate_sems)
    start_all(copies)
    wait_all(copies)
    gain_out[...] = jnp.zeros_like(gain_out)
    tile = tile_of(own, 128)

    def step(index, carry):
        start = pl.multiple_of(index * tile, 16)
        grad = dot_nt(grad_ref[pl.ds(start, tile), :width], value_weight[...])
        grad = grad + dot_nt(grad_ref[pl.ds(start, tile), width:], gate_weight[...])
        normed, inverse = row_stats(res_ref[pl.ds(start + RIM, tile), :].astype(F32))
        term = grad * normed
        gain_out[...] += jnp.sum(term.reshape(tile // 8, 8, width), axis=0)
        scaled = grad * gain_ref[...]
        result = inverse * (
            scaled
            - jnp.mean(scaled, axis=-1, keepdims=True)
            - normed * jnp.mean(scaled * normed, axis=-1, keepdims=True)
        )
        upstream = jnp.concatenate(
            [ref[0, pl.ds(start + RIM, tile), :] for ref in up_refs], axis=1
        ).astype(F32)
        turned[...] = (upstream + result).astype(BF16)
        deal(turned, out_refs, place_ref, start)
        return carry

    lax.fori_loop(0, own // tile, step, 0)


def close_block(ids, alternate, places, upstream, grad, residual, gain, one_halves, two_halves):
    parts, rows, local = upstream.shape
    own, width = grad.shape[0], residual.shape[1]
    slots = ids.shape[0]

    def up_spec(source):
        return pl.BlockSpec((1, rows, local), lambda i, a, b, place: (place[source], 0, 0))

    return pl.pallas_call(
        functools.partial(close_kernel, parts, len(one_halves)),
        grid_spec=pltpu.PrefetchScalarGridSpec(
            num_scalar_prefetch=3,
            grid=(1,),
            in_specs=[up_spec(s) for s in range(parts)] + [VMEM_SPEC] * 3
            + [ANY_SPEC] * (2 * len(one_halves)),
            out_specs=[VMEM_SPEC] * (parts + 1),
            scratch_shapes=[
                pltpu.VMEM((width, width), BF16),
                pltpu.VMEM((width, width), BF16),
                pltpu.VMEM((tile_of(own, 128), width), BF16),
                pltpu.SemaphoreType.DMA((slots,)),
                pltpu.SemaphoreType.DMA((slots,)),
            ],
        ),
        out_shape=[jax.ShapeDtypeStruct((own, width // parts), BF16)] * parts
        + [jax.ShapeDtypeStruct((8, width), F32)],
        cost_estimate=cost(4 * own * width * width, 30 * own * width),
        name="close_block",
    )(
        ids,
        alternate,
        places,
        *([upstream] * parts),
        grad,
        residual,
        gain,
        *one_halves,
        *two_halves,
    )


def after(value, *others):
    return lax.optimization_barrier((value, others))[0]


def flip(cells, bit):
    count = lax.axis_size("tm")
    return lax.ppermute(cells, "tm", [(i, i ^ bit) for i in range(count)])


def join(pair, *others):
    return jnp.concatenate(lax.optimization_barrier((tuple(pair), others))[0], axis=0)


def slot_order(bits):
    order = []
    for slot in range(lax.axis_size("tm")):
        order.append(sum(bit for level, bit in enumerate(bits) if (slot >> level) & 1))
    return lax.axis_index("tm").astype(jnp.int32) ^ jnp.asarray(order, jnp.int32)


def tm_pairs():
    count = lax.axis_size("tm")
    pairs = []
    for i in range(1, count - 1, 2):
        pairs += [(i, i + 1), (i + 1, i)]
    return pairs


def send_heads(pieces):
    count = lax.axis_size("head")
    result = [pieces[0]]
    for shift in range(1, count):
        result.append(
            lax.ppermute(pieces[shift], "head", [(i, (i + shift) % count) for i in range(count)])
        )
    return result


def rim_pieces(rows, count_rims):
    heads, count = lax.axis_size("head"), lax.axis_size("tm")
    me = lax.axis_index("head")
    result = []
    for j in range(count_rims):
        pairs = []
        for i in range(count - 1):
            pairs.append((j * count + i, i + 1))
            pairs.append(((heads - 1 - j) * count + i + 1, (heads - 1) * count + i))
        piece = jnp.where(me == j, rows[-RIM:], rows[:RIM])
        result.append(lax.ppermute(piece, ("head", "tm"), pairs))
    return result


def window_of(rows, head, conv_rows):
    return lax.dynamic_slice_in_dim(
        rows,
        jnp.clip(head * conv_rows - RIM, 0, rows.shape[0] - conv_rows - 2 * RIM),
        conv_rows + 2 * RIM,
        0,
    )


def with_rim(window, rim_first, rim_last):
    me, heads = lax.axis_index("head"), lax.axis_size("head")
    first = jnp.concatenate([rim_first, window[:-RIM]], axis=0)
    last = jnp.concatenate([window[RIM:], rim_last], axis=0)
    return jnp.where(me == 0, first, jnp.where(me == heads - 1, last, window))


def all_heads(rows, conv_rows):
    me, heads = lax.axis_index("head"), lax.axis_size("head")
    pieces = send_heads(
        [window_of(rows, (me + shift) % heads, conv_rows) for shift in range(heads)]
    )
    rims = rim_pieces(rows, heads)
    result = []
    for shift, piece in enumerate(pieces):
        result.append(with_rim(piece, rims[-shift % heads], rims[shift]))
    return jnp.stack(result, 0)


def in_order(parts):
    count = len(parts)
    me = lax.axis_index("head")
    if count == 2:
        return jnp.where(
            me == 0,
            jnp.concatenate(parts, axis=0),
            jnp.concatenate(parts[::-1], axis=0),
        )
    stacked = jnp.stack(parts, 0)
    ordered = jnp.take(stacked, (me - jnp.arange(count)) % count, axis=0)
    return ordered.reshape((-1,) + parts[0].shape[1:])


def on_device(
    frames,
    segment_lengths,
    attn_gain,
    qkv_proj,
    out_proj,
    logit_scale,
    conv_gain,
    glu_proj,
    kernel,
    post_gain,
    mix_proj,
    cotangent,
):
    head_count = lax.axis_size("head")
    shard_count = lax.axis_size("tm")
    head_place = lax.axis_index("head")
    shard_place = lax.axis_index("tm")
    local_frames, width = frames.shape
    conv_rows = local_frames // head_count
    local_width = qkv_proj.shape[2]
    all_frames = local_frames * shard_count
    devices = head_count * shard_count
    bits = []
    bit = shard_count // 2
    while bit:
        bits.append(bit)
        bit //= 2
    other_bits = bits[-2:-1] + bits[:-2] + bits[-1:]
    ids = slot_order(bits)
    alternate = slot_order(other_bits)
    places = ((head_place - jnp.arange(head_count)) % head_count).astype(jnp.int32)

    last_bit = bits[-1]
    even = shard_place % 2 == 0
    key_value_cells = jnp.concatenate([qkv_proj[:, 1], qkv_proj[:, 2]], axis=1)
    query_cells = qkv_proj[:, 0]
    normed = None
    for level in range(len(bits) - 2):
        arrived = (flip(key_value_cells, bits[level]), flip(query_cells, other_bits[level]))
        if level == 0:
            arrived = lax.optimization_barrier(arrived)
            normed = norm_rows(after(frames, arrived), attn_gain[None, :])
            out_shard, glu_shard, mix_shard, _ = lax.optimization_barrier(
                (out_proj, glu_proj, mix_proj, arrived)
            )
            one_cells = jnp.concatenate([out_shard.T, glu_shard[:, :width]], axis=1)
            two_cells = jnp.concatenate([glu_shard[:, width:], mix_shard], axis=1)
            two_pair = (two_cells, flip(two_cells, other_bits[0]))
        else:
            arrived = lax.optimization_barrier(arrived + (normed,))
            normed = arrived[2]
        key_value_cells = jnp.concatenate([key_value_cells, arrived[0]], axis=0)
        query_cells = jnp.concatenate([query_cells, arrived[1]], axis=0)
    gathering = arrived[:2]
    one_pair = (one_cells, flip(after(one_cells, gathering), bits[0]))
    segment_lengths, logit_scale, kernel, _ = lax.optimization_barrier(
        (segment_lengths, logit_scale, kernel, gathering)
    )
    ends = jnp.cumsum(segment_lengths).astype(jnp.int32)

    def segment_of(positions):
        located = jnp.sum((ends[None, :] <= positions[:, None]).astype(jnp.int32), axis=1)
        return jnp.where(positions < 0, -1, located)

    scale = jnp.repeat(logit_scale * (math.log2(math.e) / HD), HD)[None, :]
    base = shard_place * local_frames
    own_positions = base + jnp.arange(local_frames, dtype=jnp.int32)
    halo_positions = jnp.concatenate(
        [base - MOST + jnp.arange(MOST), base + local_frames + jnp.arange(MOST)]
    ).astype(jnp.int32)
    own_segment, halo_segment = segment_of(own_positions), segment_of(halo_positions)
    block = tile_of(local_frames, 256)
    blocks = local_frames // block
    first_frame = base + block * jnp.arange(blocks, dtype=jnp.int32)
    last_frame = first_frame + block - 1
    low = jnp.max(jnp.where(ends[None, :] <= first_frame[:, None], ends[None, :], 0), axis=1)
    high = jnp.min(
        jnp.where(ends[None, :] > last_frame[:, None], ends[None, :], 2 * all_frames), axis=1
    )
    low, high = low - base, high - base

    def key_range(least, most, rows, offset):
        start = (jnp.clip(least, 0, rows) // LANE) * LANE
        count = jnp.maximum((most - start + KEYS - 1) // KEYS, 0)
        start = jnp.maximum(jnp.minimum(start, rows - KEYS * count), 0)
        return offset + start, count

    own_start, own_count = key_range(low, jnp.clip(high, 0, local_frames), local_frames, 0)
    before_start, before_count = key_range(
        low + MOST, jnp.where(low < 0, MOST, -KEYS), MOST, 0
    )
    after_start, after_count = key_range(
        0 * high, jnp.clip(high - local_frames, -KEYS, MOST), MOST, MOST
    )
    halo_start = jnp.where(before_count > 0, before_start, after_start)
    halo_count = jnp.where(before_count > 0, before_count, after_count)
    conv_all = conv_rows + 2 * RIM
    conv_first = base + head_place * conv_rows - RIM
    limits = jnp.concatenate([jnp.zeros((1,), jnp.int32), ends])
    limits = jnp.concatenate(
        [
            jnp.clip(limits - conv_first, 0, conv_all),
            jnp.sum((ends <= conv_first).astype(jnp.int32), keepdims=True),
            jnp.sum((limits[:-1] < conv_first + conv_all).astype(jnp.int32), keepdims=True),
        ]
    )
    taps = kernel.reshape(KERNEL * (width // LANE), LANE)

    (
        from_x, own_start, own_count, halo_start, halo_count, own_segment, halo_segment,
        limits, scale, taps,
    ) = lax.optimization_barrier(
        (
            (flip(key_value_cells, bits[-2]), flip(query_cells, other_bits[-2])),
            own_start, own_count, halo_start, halo_count, own_segment, halo_segment,
            limits, scale, taps,
        )
    )
    arrived = from_x
    key_value_pieces = (key_value_cells, arrived[0])
    query_pieces = (query_cells, arrived[1])
    key_value_pieces += tuple(flip(cells, last_bit) for cells in key_value_pieces)
    query_pieces += tuple(flip(cells, last_bit) for cells in query_pieces)
    evens = jnp.reshape(even.astype(jnp.int32), (1,))
    key_value, queries, near, away = project(
        ids, alternate, evens, normed, key_value_pieces, query_pieces, scale
    )
    near = flip(near, 1)
    away = lax.ppermute(away, "tm", tm_pairs())
    upstream = all_heads(after(cotangent, queries), conv_rows)
    frame_rims = rim_pieces(after(frames, queries), 1)[0]
    frame_rows = with_rim(window_of(frames, head_place, conv_rows), frame_rims, frame_rims)

    one_cells, two_cells = join(one_pair, queries), join(two_pair, queries)
    one_pair = (one_cells, flip(one_cells, bits[1]))
    two_pair = (two_cells, flip(two_cells, other_bits[1]))
    for level in range(2, len(bits) - 2):
        one_cells, two_cells = join(one_pair, queries), join(two_pair, queries)
        one_pair = (one_cells, flip(one_cells, bits[level]))
        two_pair = (two_cells, flip(two_cells, other_bits[level]))
    own_sums = attend_own(own_start, own_count, queries, key_value, own_segment)
    one_cells, two_cells = join(one_pair, own_sums), join(two_pair, own_sums)
    one_pair = (one_cells, flip(one_cells, bits[-2]))
    two_pair = (two_cells, flip(two_cells, other_bits[-2]))
    heads_out = attend_rest(
        halo_start,
        halo_count,
        evens,
        queries,
        near,
        away,
        own_segment,
        halo_segment,
        own_sums,
    )
    heads_all = all_heads(after(heads_out, upstream), conv_rows)
    one_halves = one_pair + tuple(flip(after(c, heads_out), last_bit) for c in one_pair)
    two_halves = two_pair + tuple(flip(after(c, heads_out), last_bit) for c in two_pair)
    residual, gated, value, gate = open_block(
        ids, alternate, places, heads_all, frame_rows, conv_gain[None, :], one_halves, two_halves
    )
    *out_parts, depth_grad, post_sum = middle_block(
        alternate,
        places,
        limits,
        upstream,
        gated,
        residual,
        taps,
        post_gain[None, :],
        two_halves,
    )
    out_frames = in_order(send_heads(out_parts))
    glu_grad, taps_sum = spread_block(limits, depth_grad, gated, value, gate, taps)
    tap_rows = taps_sum.reshape(KERNEL, width)
    first_terms = jnp.concatenate([tap_rows, jnp.sum(post_sum, axis=0, keepdims=True)], axis=0)
    scattered = lax.all_to_all(
        first_terms.reshape(devices, (KERNEL + 1) * width // devices),
        ("head", "tm"),
        split_axis=0,
        concat_axis=0,
        tiled=True,
    )
    share = jnp.sum(scattered, axis=0)
    *grad_parts, open_sum = close_block(
        ids,
        alternate,
        places,
        upstream,
        glu_grad,
        residual,
        conv_gain[None, :],
        one_halves,
        two_halves,
    )
    grad_parts[0] = after(grad_parts[0], out_frames)
    grad_input = in_order(send_heads(grad_parts))
    last_terms = jnp.concatenate([share, jnp.sum(open_sum, axis=0)], axis=0)
    everywhere = lax.all_to_all(
        jnp.broadcast_to(last_terms[None], (devices, last_terms.shape[0])),
        ("head", "tm"),
        split_axis=0,
        concat_axis=0,
        tiled=True,
    )
    grad_scale = 1.0 / math.sqrt(all_frames)
    reduced = everywhere[:, : share.shape[0]].reshape(KERNEL + 1, width)
    open_total = jnp.sum(everywhere[:, share.shape[0] :], axis=0)
    gains = jnp.stack([open_total, reduced[KERNEL]], axis=0)
    return (out_frames, grad_input, reduced[:KERNEL] * grad_scale, gains * grad_scale)


def solution(mesh):
    placed = (
        P("tm", None),
        P(),
        P(),
        P("tm", None, "head"),
        P(None, "tm"),
        P("head"),
        P(),
        P("tm", None),
        P(),
        P(),
        P("tm", None),
        P("tm", "head"),
    )
    return jax.shard_map(
        on_device,
        mesh=mesh,
        in_specs=placed,
        out_specs=(P("tm", "head"), P("tm", "head"), P(), P()),
        check_vma=False,
    )
```

```python
import functools
import math

import jax
import jax.numpy as jnp
from jax import lax
from jax.experimental import pallas as pl
from jax.experimental.pallas import tpu as pltpu
from jax.sharding import PartitionSpec as P

HD = 64
KERNEL = 31
HALF = 15
MOST = 512
LANE = 128
RIM = 32
EDGE = 16
KEYS = 256

EPS_NORM = 1e-05
EPS_HEAD = 1e-06


F32 = jnp.float32
BF16 = jnp.bfloat16
VMEM_SPEC = pl.BlockSpec(memory_space=pltpu.VMEM)
ANY_SPEC = pl.BlockSpec(memory_space=pltpu.HBM)
SMEM_SPEC = pl.BlockSpec(memory_space=pltpu.SMEM)


def tile_of(count, most):
    best = 16
    for size in range(16, most + 1, 16):
        if count % size == 0:
            best = size
    return best


def dot_nn(a, b):
    return lax.dot_general(a, b, (((1,), (0,)), ((), ())), preferred_element_type=F32)


def dot_nt(a, b):
    return lax.dot_general(a, b, (((1,), (1,)), ((), ())), preferred_element_type=F32)


def row_stats(values):
    average = jnp.mean(values, axis=-1, keepdims=True)
    centred = values - average
    inverse = lax.rsqrt(jnp.mean(centred * centred, axis=-1, keepdims=True) + EPS_NORM)
    return centred * inverse, inverse


def slot_copies(ids_ref, halves, target, sems, column=0):
    slots = ids_ref.shape[0]
    each = slots // len(halves)
    rows = target.shape[0] // slots
    columns = pl.ds(column, target.shape[1])
    copies = []
    for slot in range(slots):
        source = halves[slot // each].at[pl.ds((slot % each) * rows, rows), columns]
        place = pl.multiple_of(ids_ref[slot] * rows, rows)
        copies.append(
            pltpu.make_async_copy(source, target.at[pl.ds(place, rows), :], sems.at[slot])
        )
    return copies


def start_all(copies):
    for copy in copies:
        copy.start()


def wait_all(copies):
    for copy in copies:
        copy.wait()


def cost(flops, moved):
    return pl.CostEstimate(flops=flops, transcendentals=0, bytes_accessed=moved)


def norm_kernel(x_ref, gain_ref, out_ref):
    normed, _ = row_stats(x_ref[...].astype(F32))
    out_ref[...] = (normed * gain_ref[...]).astype(BF16)


def norm_rows(x, gain):
    rows, width = x.shape
    tile = tile_of(rows, 256)
    return pl.pallas_call(
        norm_kernel,
        grid=(rows // tile,),
        in_specs=[
            pl.BlockSpec((tile, width), lambda i: (i, 0)),
            pl.BlockSpec((1, width), lambda i: (0, 0)),
        ],
        out_specs=pl.BlockSpec((tile, width), lambda i: (i, 0)),
        out_shape=jax.ShapeDtypeStruct((rows, width), BF16),
        cost_estimate=cost(0, 12 * rows * width),
        name="norm_rows",
    )(x, gain)


def qkv_kernel(pieces, ids_ref, alt_ref, even_ref, x_ref, scale_ref, *refs):
    kv_refs, q_refs, refs = refs[:pieces], refs[pieces : 2 * pieces], refs[2 * pieces :]
    kv_out, q_out, near_out, away_out = refs[:4]
    k_weight, v_weight, q_weight, k_sems, v_sems, q_sems = refs[4:]
    first = pl.program_id(0) == 0
    k_copies = slot_copies(ids_ref, kv_refs, k_weight, k_sems)
    v_copies = slot_copies(
        ids_ref, kv_refs, v_weight, v_sems, k_weight.shape[1]
    )
    q_copies = slot_copies(alt_ref, q_refs, q_weight, q_sems)

    @pl.when(first)
    def _():
        start_all(k_copies + v_copies + q_copies)
        wait_all(k_copies)

    x = x_ref[...]
    width = k_weight.shape[1]
    group = min(KEYS, width)
    row_head = lax.broadcasted_iota(jnp.int32, (group, group), 0) // HD
    column_head = lax.broadcasted_iota(jnp.int32, (group, group), 1) // HD
    ones = jnp.where(row_head == column_head, 1.0, 0.0).astype(BF16)

    def unit(product, out, scale):
        for start in range(0, width, group):
            part = product[:, start : start + group]
            total = dot_nn((part * part).astype(BF16), ones)
            scaled = part * lax.rsqrt(total * (1.0 / HD) + EPS_HEAD)
            if scale is not None:
                scaled = scaled * scale[:, start : start + group]
            out[:, start : start + group] = scaled.astype(BF16)

    unit(dot_nn(x, k_weight[...]), kv_out, None)

    @pl.when(first)
    def _():
        wait_all(v_copies)

    kv_out[:, width:] = dot_nn(x, v_weight[...]).astype(BF16)

    @pl.when(first)
    def _():
        wait_all(q_copies)

    step, last = pl.program_id(0), pl.num_programs(0) - 1
    is_even = even_ref[0] == 1

    @pl.when(((step == last) & is_even) | ((step == 0) & jnp.logical_not(is_even)))
    def _():
        near_out[...] = kv_out[...]

    @pl.when(((step == 0) & is_even) | ((step == last) & jnp.logical_not(is_even)))
    def _():
        away_out[...] = kv_out[...]

    unit(dot_nn(x, q_weight[...]), q_out, scale_ref)


def project(ids, alternate, even, x, key_value_pieces, query_pieces, scale):
    rows, width = x.shape
    columns = query_pieces[0].shape[1]
    slots = ids.shape[0]
    tile = MOST
    pieces = len(query_pieces)
    return pl.pallas_call(
        functools.partial(qkv_kernel, pieces),
        grid_spec=pltpu.PrefetchScalarGridSpec(
            num_scalar_prefetch=3,
            grid=(rows // tile,),
            in_specs=[
                pl.BlockSpec((tile, width), lambda i, a, b, c: (i, 0)),
                pl.BlockSpec((1, columns), lambda i, a, b, c: (0, 0)),
            ]
            + [ANY_SPEC] * (2 * pieces),
            out_specs=[
                pl.BlockSpec((tile, 2 * columns), lambda i, a, b, c: (i, 0)),
                pl.BlockSpec((tile, columns), lambda i, a, b, c: (i, 0)),
                pl.BlockSpec((tile, 2 * columns), lambda i, a, b, c: (0, 0)),
                pl.BlockSpec((tile, 2 * columns), lambda i, a, b, c: (0, 0)),
            ],
            scratch_shapes=[pltpu.VMEM((width, columns), BF16)] * 3
            + [pltpu.SemaphoreType.DMA((slots,))] * 3,
        ),
        out_shape=[
            jax.ShapeDtypeStruct((rows, 2 * columns), BF16),
            jax.ShapeDtypeStruct((rows, columns), BF16),
            jax.ShapeDtypeStruct((tile, 2 * columns), BF16),
            jax.ShapeDtypeStruct((tile, 2 * columns), BF16),
        ],
        cost_estimate=cost(6 * rows * width * columns, 12 * width * width),
        name="project",
    )(ids, alternate, even, x, scale, *key_value_pieces, *query_pieces)


def attend_step(acc, q_ref, kv_ref, qseg_ref, kseg_ref, bias_ref, start):
    rows, width = q_ref.shape
    lane = lax.broadcasted_iota(jnp.int32, (rows, LANE), 1)
    lane_keys = lax.broadcasted_iota(jnp.int32, (KEYS, LANE), 1)
    same = qseg_ref[...] == kseg_ref[:, pl.ds(start, KEYS)]
    bias_ref[...] = jnp.where(same, 0.0, -1e30)
    for pair in range(width // LANE):
        queries = q_ref[:, pl.ds(pair * LANE, LANE)]
        keys = kv_ref[pl.ds(start, KEYS), pl.ds(pair * LANE, LANE)]
        values = kv_ref[pl.ds(start, KEYS), pl.ds(width + pair * LANE, LANE)]
        for side in range(2):
            mine = (lane < HD) if side == 0 else (lane >= HD)
            mine_keys = (lane_keys < HD) if side == 0 else (lane_keys >= HD)
            one = jnp.where(mine, queries, jnp.zeros_like(queries))
            scores = dot_nt(one, keys) + bias_ref[...]
            weights = jnp.exp2(scores).astype(BF16)
            extended = jnp.where(mine_keys, values, jnp.ones_like(values))
            acc[2 * pair + side] += dot_nn(weights, extended)


def attend_own_kernel(first_ref, count_ref, q_ref, kv_ref, qseg_ref, kseg_ref, acc_ref, bias_ref):
    block = pl.program_id(0)
    acc_ref[...] = jnp.zeros_like(acc_ref)

    def step(index, carry):
        start = pl.multiple_of(first_ref[block] + index * KEYS, LANE)
        attend_step(acc_ref, q_ref, kv_ref, qseg_ref, kseg_ref, bias_ref, start)
        return carry

    lax.fori_loop(0, count_ref[block], step, 0)


def attend_rest_kernel(
    first_ref, count_ref, even_ref, q_ref, near_ref, away_ref, qseg_ref, kseg_ref, own_ref,
    out_ref, acc_ref, bias_ref, kv_ref, sems,
):
    half = near_ref.shape[0]
    near_place = pl.multiple_of(even_ref[0] * half, half)
    away_place = pl.multiple_of((1 - even_ref[0]) * half, half)

    @pl.when(pl.program_id(0) == 0)
    def _():
        copies = [
            pltpu.make_async_copy(near_ref, kv_ref.at[pl.ds(near_place, half), :], sems.at[0]),
            pltpu.make_async_copy(away_ref, kv_ref.at[pl.ds(away_place, half), :], sems.at[1]),
        ]
        start_all(copies)
        wait_all(copies)

    block = pl.program_id(0)
    rows, width = q_ref.shape
    lane = lax.broadcasted_iota(jnp.int32, (rows, LANE), 1)

    def finish(acc):
        for pair in range(width // LANE):
            even, odd = acc[2 * pair], acc[2 * pair + 1]
            above = jnp.where(lane < HD, even, odd)
            below = pltpu.roll(jnp.where(lane < HD, odd, even), HD, 1)
            out_ref[:, pl.ds(pair * LANE, LANE)] = (above / below).astype(BF16)

    def step(index, carry):
        start = pl.multiple_of(first_ref[block] + index * KEYS, LANE)
        attend_step(acc_ref, q_ref, kv_ref, qseg_ref, kseg_ref, bias_ref, start)
        return carry

    @pl.when(count_ref[block] == 0)
    def _():
        finish(own_ref)

    @pl.when(count_ref[block] > 0)
    def _():
        acc_ref[...] = own_ref[...]
        lax.fori_loop(0, count_ref[block], step, 0)
        finish(acc_ref)


def attend_own(first, count, queries, key_value, segment):
    rows, width = queries.shape
    block = rows // first.shape[0]
    heads = width // HD
    return pl.pallas_call(
        attend_own_kernel,
        grid_spec=pltpu.PrefetchScalarGridSpec(
            num_scalar_prefetch=2,
            grid=(rows // block,),
            in_specs=[
                pl.BlockSpec((block, width), lambda i, a, b: (i, 0)),
                pl.BlockSpec((rows, 2 * width), lambda i, a, b: (0, 0)),
                pl.BlockSpec((block, 1), lambda i, a, b: (i, 0)),
                pl.BlockSpec((1, rows), lambda i, a, b: (0, 0)),
            ],
            out_specs=pl.BlockSpec((heads, block, LANE), lambda i, a, b: (0, i, 0)),
            scratch_shapes=[pltpu.VMEM((block, KEYS), F32)],
        ),
        out_shape=jax.ShapeDtypeStruct((heads, rows, LANE), F32),
        cost_estimate=cost(16 * rows * width * width, 20 * rows * width),
        name="attend_own",
    )(first, count, queries, key_value, segment[:, None], segment[None, :])


def attend_rest(first, count, even, queries, near, away, segment, key_segment, own):
    rows, width = queries.shape
    block = rows // first.shape[0]
    heads = width // HD
    keys = 2 * near.shape[0]
    return pl.pallas_call(
        attend_rest_kernel,
        grid_spec=pltpu.PrefetchScalarGridSpec(
            num_scalar_prefetch=3,
            grid=(rows // block,),
            in_specs=[
                pl.BlockSpec((block, width), lambda i, a, b, c: (i, 0)),
                ANY_SPEC,
                ANY_SPEC,
                pl.BlockSpec((block, 1), lambda i, a, b, c: (i, 0)),
                pl.BlockSpec((1, keys), lambda i, a, b, c: (0, 0)),
                pl.BlockSpec((heads, block, LANE), lambda i, a, b, c: (0, i, 0)),
            ],
            out_specs=pl.BlockSpec((block, width), lambda i, a, b, c: (i, 0)),
            scratch_shapes=[
                pltpu.VMEM((heads, block, LANE), F32),
                pltpu.VMEM((block, KEYS), F32),
                pltpu.VMEM((keys, 2 * width), BF16),
                pltpu.SemaphoreType.DMA((2,)),
            ],
        ),
        out_shape=jax.ShapeDtypeStruct((rows, width), BF16),
        cost_estimate=cost(4 * rows * width * width, 20 * rows * width),
        name="attend_rest",
    )(first, count, even, queries, near, away, segment[:, None], key_segment[None, :], own)


def open_kernel(
    parts, slabs, ids_ref, alt_ref, place_ref, *refs
):
    heads_refs = refs[:parts]
    (frames_ref, gain_ref) = refs[parts : parts + 2]
    refs = refs[parts + 2 :]
    ones, twos, refs = refs[:slabs], refs[slabs : 2 * slabs], refs[2 * slabs :]
    (res_ref, gated_ref, value_ref, gate_ref) = refs[:4]
    out_weight, value_weight, gate_weight, out_sems, value_sems, gate_sems = refs[4:]

    width = frames_ref.shape[1]
    first = pl.program_id(0) == 0
    out_copies = slot_copies(ids_ref, ones, out_weight, out_sems)
    glu_copies = slot_copies(ids_ref, ones, value_weight, value_sems, width)
    glu_copies += slot_copies(alt_ref, twos, gate_weight, gate_sems)

    @pl.when(first)
    def _():
        start_all(out_copies + glu_copies)
        wait_all(out_copies)

    heads = jnp.concatenate([ref[0] for ref in heads_refs], axis=1)
    total = frames_ref[...].astype(F32) + dot_nt(heads, out_weight[...])
    residual = total.astype(BF16)
    res_ref[...] = residual
    normed, _ = row_stats(residual.astype(F32))
    conv_input = (normed * gain_ref[...]).astype(BF16)

    @pl.when(first)
    def _():
        wait_all(glu_copies)

    value = dot_nn(conv_input, value_weight[...])
    gate = jax.nn.sigmoid(dot_nn(conv_input, gate_weight[...]))
    value_ref[...] = value.astype(BF16)
    gate_ref[...] = gate.astype(BF16)
    gated_ref[...] = (value * gate).astype(BF16)


def open_block(ids, alternate, places, heads, frames, gain, one_halves, two_halves):
    parts, rows, local = heads.shape
    width = frames.shape[1]
    tile = tile_of(rows, 288)
    slots = ids.shape[0]

    def head_spec(source):
        return pl.BlockSpec((1, tile, local), lambda i, a, b, place: (place[source], i, 0))

    row_spec = pl.BlockSpec((tile, width), lambda i, a, b, place: (i, 0))
    return pl.pallas_call(
        functools.partial(open_kernel, parts, len(one_halves)),
        grid_spec=pltpu.PrefetchScalarGridSpec(
            num_scalar_prefetch=3,
            grid=(rows // tile,),
            in_specs=[head_spec(s) for s in range(parts)]
            + [row_spec, pl.BlockSpec((1, width), lambda i, a, b, place: (0, 0))]
            + [ANY_SPEC] * (2 * len(one_halves)),
            out_specs=[row_spec] * 4,
            scratch_shapes=[
                pltpu.VMEM((width, width), BF16),
                pltpu.VMEM((width, width), BF16),
                pltpu.VMEM((width, width), BF16),
                pltpu.SemaphoreType.DMA((slots,)),
                pltpu.SemaphoreType.DMA((slots,)),
                pltpu.SemaphoreType.DMA((slots,)),
            ],
        ),
        out_shape=[
            jax.ShapeDtypeStruct((rows, width), BF16),
            jax.ShapeDtypeStruct((rows, width), BF16),
            jax.ShapeDtypeStruct((rows, width), BF16),
            jax.ShapeDtypeStruct((rows, width), BF16),
        ],
        cost_estimate=cost(10 * rows * width * width, 24 * rows * width),
        name="open_block",
    )(ids, alternate, places, *([heads] * parts), frames, gain, *one_halves, *two_halves)


SUB = 8
STEP = 8
SPAN = STEP + KERNEL - 1
LEAD = 16


def at_frame(frame, frames=1, tile=SUB):
    start = frame * tile
    if not isinstance(start, int):
        start = pl.multiple_of(start, SUB)
    return pl.ds(start, frames * tile)


def to_frames(source_ref, target, count, shift):
    width = source_ref.shape[1]
    tile = width // LANE

    def step(index, carry):
        start = pl.multiple_of(index * 16, 16)
        for block in range(tile):
            values = source_ref[pl.ds(start, 16), block * LANE : (block + 1) * LANE].astype(F32)
            target[pl.ds((start + shift) * tile + block, 16, stride=tile), :] = values
        return carry

    lax.fori_loop(0, count // 16, step, 0)


def copy_frames(source, target, first, place, count, tile):
    def step(index, carry):
        source_at = at_frame(first + index * STEP, STEP, tile)
        target[at_frame(place + index * STEP, STEP, tile), :] = source[source_at, :]
        return carry

    lax.fori_loop(0, (count + STEP - 1) // STEP, step, 0)


def deal(rows_ref, out_refs, place_ref, start):
    parts = len(out_refs)
    rows, width = rows_ref.shape
    local = width // parts
    for shift, out_ref in enumerate(out_refs):
        head = lax.rem(place_ref[0] + shift, parts)
        columns = pl.ds(pl.multiple_of(head * local, local), local)
        out_ref[pl.ds(start, rows), :] = rows_ref[:, columns]


def middle_kernel(parts, slabs, ids_ref, place_ref, limits_ref, *refs):
    up_refs = refs[:parts]
    (gated_ref, res_ref, taps_ref, gain_ref) = refs[parts : parts + 4]
    refs = refs[parts + 4 :]
    twos, out_refs, refs = refs[:slabs], refs[slabs : slabs + parts], refs[slabs + parts :]
    (grad_ref, gain_out, cells, buffer, depth, back, swished, mix, turned, sems) = refs
    rows, width = gated_ref.shape
    blocks = width // LANE
    inner = rows - 2 * EDGE
    own = rows - 2 * RIM

    copies = slot_copies(ids_ref, twos, mix, sems, width)
    start_all(copies)

    depth[...] = jnp.zeros_like(depth)
    buffer[at_frame(0, LEAD, blocks), :] = jnp.zeros((LEAD * blocks, LANE), F32)
    to_frames(gated_ref, cells, rows, 0)
    segments = limits_ref.shape[0] - 3

    def segment_step(segment, carry):
        first, last = limits_ref[segment], limits_ref[segment + 1]
        length = last - first
        copy_frames(cells, buffer, first, LEAD, length, blocks)
        zeros = jnp.zeros(((LEAD + STEP) * blocks, LANE), F32)
        buffer[at_frame(LEAD + length, LEAD + STEP, blocks), :] = zeros

        def convolve(index, carry):
            start = index * STEP
            sums = [None] * STEP
            for near in range(SPAN):
                frame = buffer[at_frame(start + LEAD - HALF + near, 1, blocks), :]
                for one in range(STEP):
                    tap = near - one
                    if 0 <= tap < KERNEL:
                        term = taps_ref[tap * blocks : (tap + 1) * blocks, :] * frame
                        sums[one] = term if sums[one] is None else sums[one] + term
            for one in range(STEP):
                depth[at_frame(first + start + one, 1, blocks), :] = sums[one]
            return carry

        lax.fori_loop(0, (length + STEP - 1) // STEP, convolve, 0)
        return carry

    lax.fori_loop(limits_ref[segments + 1], limits_ref[segments + 2], segment_step, 0)

    wait_all(copies)

    big = tile_of(inner, 288)

    def backward(index, carry):
        start = pl.multiple_of(index * big, 16)
        upstream = jnp.concatenate(
            [ref[0, pl.ds(start + EDGE, big), :] for ref in up_refs], axis=1
        )
        back[pl.ds(start, big), :] = dot_nt(upstream, mix[...])
        return carry

    lax.fori_loop(0, inner // big, backward, 0)
    gain_out[...] = jnp.zeros_like(gain_out)

    def pointwise(index, carry):
        start = pl.multiple_of(index * 16, 16)
        cuts = [slice(b * LANE, (b + 1) * LANE) for b in range(blocks)]
        values = [
            depth[pl.ds((start + EDGE) * blocks + b, 16, stride=blocks), :] for b in range(blocks)
        ]
        average = jnp.sum(functools.reduce(jnp.add, values), axis=1, keepdims=True) / width
        values = [v - average for v in values]
        spread_of = (
            jnp.sum(functools.reduce(jnp.add, [v * v for v in values]), axis=1, keepdims=True)
            / width
        )
        inverse = lax.rsqrt(spread_of + EPS_NORM)
        scaled, first_sum, second_sum = [], 0.0, 0.0
        is_own = jnp.where((index >= 1) & (index < 1 + own // 16), 1.0, 0.0)
        for b in range(blocks):
            normed = values[b] * inverse
            post = normed * gain_ref[:, cuts[b]]
            gate = jax.nn.sigmoid(post)
            swished[pl.ds(start, 16), cuts[b]] = (post * gate).astype(BF16)
            grad = back[pl.ds(start, 16), cuts[b]] * (gate * (1.0 + post * (1.0 - gate)))
            term = grad * normed
            gain_out[:, cuts[b]] += (term[:8] + term[8:]) * is_own
            part = grad * gain_ref[:, cuts[b]]
            scaled.append(part)
            first_sum = first_sum + part
            second_sum = second_sum + part * normed
            values[b] = normed
        first_mean = jnp.sum(first_sum, axis=1, keepdims=True) / width
        second_mean = jnp.sum(second_sum, axis=1, keepdims=True) / width
        for b in range(blocks):
            grad_ref[pl.ds(start, 16), cuts[b]] = (
                inverse * (scaled[b] - first_mean - values[b] * second_mean)
            ).astype(BF16)
        return carry

    lax.fori_loop(0, inner // 16, pointwise, 0)

    big = tile_of(own, 256)

    def forward(index, carry):
        start = pl.multiple_of(index * big, 16)
        product = dot_nn(swished[pl.ds(start + EDGE, big), :], mix[...])
        turned[...] = (res_ref[pl.ds(start + RIM, big), :].astype(F32) + product).astype(BF16)
        deal(turned, out_refs, place_ref, start)
        return carry

    lax.fori_loop(0, own // big, forward, 0)


def middle_block(ids, places, limits, upstream, gated, residual, taps, gain, mix_halves):
    parts, rows, local = upstream.shape
    width = gated.shape[1]
    slots = ids.shape[0]
    inner, own = rows - 2 * EDGE, rows - 2 * RIM
    blocks = width // LANE

    def up_spec(source):
        return pl.BlockSpec((1, rows, local), lambda i, a, place, b: (place[source], 0, 0))

    return pl.pallas_call(
        functools.partial(middle_kernel, parts, len(mix_halves)),
        grid_spec=pltpu.PrefetchScalarGridSpec(
            num_scalar_prefetch=3,
            grid=(1,),
            in_specs=[up_spec(s) for s in range(parts)] + [VMEM_SPEC] * 4
            + [ANY_SPEC] * len(mix_halves),
            out_specs=[VMEM_SPEC] * (parts + 2),
            scratch_shapes=[
                pltpu.VMEM(((rows + STEP) * blocks, LANE), F32),
                pltpu.VMEM(((rows + 2 * LEAD + STEP) * blocks, LANE), F32),
                pltpu.VMEM(((rows + STEP) * blocks, LANE), F32),
                pltpu.VMEM((inner, width), F32),
                pltpu.VMEM((inner, width), BF16),
                pltpu.VMEM((width, width), BF16),
                pltpu.VMEM((tile_of(own, 256), width), BF16),
                pltpu.SemaphoreType.DMA((slots,)),
            ],
        ),
        out_shape=[jax.ShapeDtypeStruct((own, width // parts), BF16)] * parts
        + [
            jax.ShapeDtypeStruct((inner, width), BF16),
            jax.ShapeDtypeStruct((8, width), F32),
        ],
        cost_estimate=cost(4 * rows * width * width, 60 * rows * width),
        name="middle_block",
    )(ids, places, limits, *([upstream] * parts), gated, residual, taps, gain, *mix_halves)


def spread_kernel(
    limits_ref, grad_ref, gated_ref, value_ref, gate_ref, taps_ref, out_ref, taps_out,
    cells, inputs, buffer, held, total,
):
    rows, width = gated_ref.shape
    blocks = width // LANE
    inner, own = rows - 2 * EDGE, rows - 2 * RIM
    taps_out[...] = jnp.zeros_like(taps_out)
    total[...] = jnp.zeros_like(total)
    buffer[at_frame(0, LEAD, blocks), :] = jnp.zeros((LEAD * blocks, LANE), F32)
    to_frames(grad_ref, cells, inner, EDGE)
    to_frames(gated_ref, inputs, rows, 0)
    segments = limits_ref.shape[0] - 3

    def segment_step(segment, carry):
        first, last = limits_ref[segment], limits_ref[segment + 1]
        own_first, own_last = jnp.maximum(first, RIM), jnp.minimum(last, rows - RIM)
        first, last = jnp.maximum(first, EDGE), jnp.minimum(last, rows - EDGE)

        @pl.when(own_last > own_first)
        def _():
            length, own_length = last - first, own_last - own_first
            skip = own_first - first
            copy_frames(cells, buffer, first, LEAD, length, blocks)
            zeros = jnp.zeros(((LEAD + STEP) * blocks, LANE), F32)
            buffer[at_frame(LEAD + length, LEAD + STEP, blocks), :] = zeros
            copy_frames(inputs, held, own_first, 0, own_length, blocks)
            held[at_frame(own_length, STEP, blocks), :] = jnp.zeros((STEP * blocks, LANE), F32)

            def convolve(index, carry):
                start = index * STEP
                sums = [None] * STEP
                mine = [held[at_frame(start + one, 1, blocks), :] for one in range(STEP)]
                terms = [None] * KERNEL
                for near in range(SPAN):
                    frame = buffer[at_frame(start + skip + LEAD - HALF + near, 1, blocks), :]
                    for one in range(STEP):
                        tap = one + KERNEL - 1 - near
                        if 0 <= tap < KERNEL:
                            place = slice(tap * blocks, (tap + 1) * blocks)
                            term = taps_ref[place, :] * frame
                            sums[one] = term if sums[one] is None else sums[one] + term
                            term = mine[one] * frame
                            terms[tap] = term if terms[tap] is None else terms[tap] + term
                    done = KERNEL - 1 + STEP - 1 - near
                    if 0 <= done < KERNEL:
                        taps_out[done * blocks : (done + 1) * blocks, :] += terms[done]
                for one in range(STEP):
                    total[at_frame(own_first + start + one, 1, blocks), :] = sums[one]
                return carry

            lax.fori_loop(0, (own_length + STEP - 1) // STEP, convolve, 0)

        return carry

    lax.fori_loop(limits_ref[segments + 1], limits_ref[segments + 2], segment_step, 0)

    def gates(index, carry):
        start = pl.multiple_of(index * 16, 16)
        for block in range(blocks):
            columns = slice(block * LANE, (block + 1) * LANE)
            gate = gate_ref[pl.ds(start + RIM, 16), columns].astype(F32)
            value = value_ref[pl.ds(start + RIM, 16), columns].astype(F32)
            through = total[pl.ds((start + RIM) * blocks + block, 16, stride=blocks), :] * gate
            out_ref[pl.ds(start, 16), columns] = through.astype(BF16)
            out_ref[pl.ds(start, 16), width + block * LANE : width + (block + 1) * LANE] = (
                through * value * (1.0 - gate)
            ).astype(BF16)
        return carry

    lax.fori_loop(0, own // 16, gates, 0)


def spread_block(limits, grad, gated, value, gate, taps):
    rows, width = gated.shape
    inner, own = rows - 2 * EDGE, rows - 2 * RIM
    blocks = width // LANE
    return pl.pallas_call(
        spread_kernel,
        grid_spec=pltpu.PrefetchScalarGridSpec(
            num_scalar_prefetch=1,
            grid=(1,),
            in_specs=[VMEM_SPEC] * 5,
            out_specs=[VMEM_SPEC] * 2,
            scratch_shapes=[
                pltpu.VMEM(((rows + STEP) * blocks, LANE), F32),
                pltpu.VMEM(((rows + STEP) * blocks, LANE), F32),
                pltpu.VMEM(((rows + 2 * LEAD + STEP) * blocks, LANE), F32),
                pltpu.VMEM(((own + 2 * STEP) * blocks, LANE), F32),
                pltpu.VMEM(((rows + STEP) * blocks, LANE), F32),
            ],
        ),
        out_shape=[
            jax.ShapeDtypeStruct((own, 2 * width), BF16),
            jax.ShapeDtypeStruct((KERNEL * blocks, LANE), F32),
        ],
        cost_estimate=cost(0, 70 * own * width),
        name="spread_block",
    )(limits, grad, gated, value, gate, taps)


def close_kernel(parts, slabs, ids_ref, alt_ref, place_ref, *refs):
    up_refs = refs[:parts]
    (grad_ref, res_ref, gain_ref) = refs[parts : parts + 3]
    refs = refs[parts + 3 :]
    ones, twos, refs = refs[:slabs], refs[slabs : 2 * slabs], refs[2 * slabs :]
    out_refs, gain_out = refs[:parts], refs[parts]
    (value_weight, gate_weight, turned, value_sems, gate_sems) = refs[parts + 1 :]
    own, width = grad_ref.shape[0], res_ref.shape[1]
    copies = slot_copies(ids_ref, ones, value_weight, value_sems, width)
    copies += slot_copies(alt_ref, twos, gate_weight, gate_sems)
    start_all(copies)
    wait_all(copies)
    gain_out[...] = jnp.zeros_like(gain_out)
    tile = tile_of(own, 128)

    def step(index, carry):
        start = pl.multiple_of(index * tile, 16)
        grad = dot_nt(grad_ref[pl.ds(start, tile), :width], value_weight[...])
        grad = grad + dot_nt(grad_ref[pl.ds(start, tile), width:], gate_weight[...])
        normed, inverse = row_stats(res_ref[pl.ds(start + RIM, tile), :].astype(F32))
        term = grad * normed
        gain_out[...] += jnp.sum(term.reshape(tile // 8, 8, width), axis=0)
        scaled = grad * gain_ref[...]
        result = inverse * (
            scaled
            - jnp.mean(scaled, axis=-1, keepdims=True)
            - normed * jnp.mean(scaled * normed, axis=-1, keepdims=True)
        )
        upstream = jnp.concatenate(
            [ref[0, pl.ds(start + RIM, tile), :] for ref in up_refs], axis=1
        ).astype(F32)
        turned[...] = (upstream + result).astype(BF16)
        deal(turned, out_refs, place_ref, start)
        return carry

    lax.fori_loop(0, own // tile, step, 0)


def close_block(ids, alternate, places, upstream, grad, residual, gain, one_halves, two_halves):
    parts, rows, local = upstream.shape
    own, width = grad.shape[0], residual.shape[1]
    slots = ids.shape[0]

    def up_spec(source):
        return pl.BlockSpec((1, rows, local), lambda i, a, b, place: (place[source], 0, 0))

    return pl.pallas_call(
        functools.partial(close_kernel, parts, len(one_halves)),
        grid_spec=pltpu.PrefetchScalarGridSpec(
            num_scalar_prefetch=3,
            grid=(1,),
            in_specs=[up_spec(s) for s in range(parts)] + [VMEM_SPEC] * 3
            + [ANY_SPEC] * (2 * len(one_halves)),
            out_specs=[VMEM_SPEC] * (parts + 1),
            scratch_shapes=[
                pltpu.VMEM((width, width), BF16),
                pltpu.VMEM((width, width), BF16),
                pltpu.VMEM((tile_of(own, 128), width), BF16),
                pltpu.SemaphoreType.DMA((slots,)),
                pltpu.SemaphoreType.DMA((slots,)),
            ],
        ),
        out_shape=[jax.ShapeDtypeStruct((own, width // parts), BF16)] * parts
        + [jax.ShapeDtypeStruct((8, width), F32)],
        cost_estimate=cost(4 * own * width * width, 30 * own * width),
        name="close_block",
    )(
        ids,
        alternate,
        places,
        *([upstream] * parts),
        grad,
        residual,
        gain,
        *one_halves,
        *two_halves,
    )


def after(value, *others):
    return lax.optimization_barrier((value, others))[0]


def flip(cells, bit):
    count = lax.axis_size("tm")
    return lax.ppermute(cells, "tm", [(i, i ^ bit) for i in range(count)])


def join(pair, *others):
    return jnp.concatenate(lax.optimization_barrier((tuple(pair), others))[0], axis=0)


def slot_order(bits):
    order = []
    for slot in range(lax.axis_size("tm")):
        order.append(sum(bit for level, bit in enumerate(bits) if (slot >> level) & 1))
    return lax.axis_index("tm").astype(jnp.int32) ^ jnp.asarray(order, jnp.int32)


def tm_pairs():
    count = lax.axis_size("tm")
    pairs = []
    for i in range(1, count - 1, 2):
        pairs += [(i, i + 1), (i + 1, i)]
    return pairs


def send_heads(pieces):
    count = lax.axis_size("head")
    result = [pieces[0]]
    for shift in range(1, count):
        result.append(
            lax.ppermute(pieces[shift], "head", [(i, (i + shift) % count) for i in range(count)])
        )
    return result


def rim_pieces(rows, count_rims):
    heads, count = lax.axis_size("head"), lax.axis_size("tm")
    me = lax.axis_index("head")
    result = []
    for j in range(count_rims):
        pairs = []
        for i in range(count - 1):
            pairs.append((j * count + i, i + 1))
            pairs.append(((heads - 1 - j) * count + i + 1, (heads - 1) * count + i))
        piece = jnp.where(me == j, rows[-RIM:], rows[:RIM])
        result.append(lax.ppermute(piece, ("head", "tm"), pairs))
    return result


def window_of(rows, head, conv_rows):
    return lax.dynamic_slice_in_dim(
        rows,
        jnp.clip(head * conv_rows - RIM, 0, rows.shape[0] - conv_rows - 2 * RIM),
        conv_rows + 2 * RIM,
        0,
    )


def with_rim(window, rim_first, rim_last):
    me, heads = lax.axis_index("head"), lax.axis_size("head")
    first = jnp.concatenate([rim_first, window[:-RIM]], axis=0)
    last = jnp.concatenate([window[RIM:], rim_last], axis=0)
    return jnp.where(me == 0, first, jnp.where(me == heads - 1, last, window))


def all_heads(rows, conv_rows):
    me, heads = lax.axis_index("head"), lax.axis_size("head")
    pieces = send_heads(
        [window_of(rows, (me + shift) % heads, conv_rows) for shift in range(heads)]
    )
    rims = rim_pieces(rows, heads)
    result = []
    for shift, piece in enumerate(pieces):
        result.append(with_rim(piece, rims[-shift % heads], rims[shift]))
    return jnp.stack(result, 0)


def in_order(parts):
    count = len(parts)
    me = lax.axis_index("head")
    if count == 2:
        return jnp.where(
            me == 0,
            jnp.concatenate(parts, axis=0),
            jnp.concatenate(parts[::-1], axis=0),
        )
    stacked = jnp.stack(parts, 0)
    ordered = jnp.take(stacked, (me - jnp.arange(count)) % count, axis=0)
    return ordered.reshape((-1,) + parts[0].shape[1:])


def on_device(
    frames,
    segment_lengths,
    attn_gain,
    qkv_proj,
    out_proj,
    logit_scale,
    conv_gain,
    glu_proj,
    kernel,
    post_gain,
    mix_proj,
    cotangent,
):
    head_count = lax.axis_size("head")
    shard_count = lax.axis_size("tm")
    head_place = lax.axis_index("head")
    shard_place = lax.axis_index("tm")
    local_frames, width = frames.shape
    conv_rows = local_frames // head_count
    local_width = qkv_proj.shape[2]
    all_frames = local_frames * shard_count
    devices = head_count * shard_count
    bits = []
    bit = shard_count // 2
    while bit:
        bits.append(bit)
        bit //= 2
    other_bits = bits[-2:-1] + bits[:-2] + bits[-1:]
    ids = slot_order(bits)
    alternate = slot_order(other_bits)
    places = ((head_place - jnp.arange(head_count)) % head_count).astype(jnp.int32)

    last_bit = bits[-1]
    even = shard_place % 2 == 0
    key_value_cells = jnp.concatenate([qkv_proj[:, 1], qkv_proj[:, 2]], axis=1)
    query_cells = qkv_proj[:, 0]
    normed = None
    for level in range(len(bits) - 2):
        arrived = (flip(key_value_cells, bits[level]), flip(query_cells, other_bits[level]))
        if level == 0:
            arrived = lax.optimization_barrier(arrived)
            normed = norm_rows(after(frames, arrived), attn_gain[None, :])
            out_shard, glu_shard, mix_shard, _ = lax.optimization_barrier(
                (out_proj, glu_proj, mix_proj, arrived)
            )
            one_cells = jnp.concatenate([out_shard.T, glu_shard[:, :width]], axis=1)
            two_cells = jnp.concatenate([glu_shard[:, width:], mix_shard], axis=1)
            two_pair = (two_cells, flip(two_cells, other_bits[0]))
        else:
            arrived = lax.optimization_barrier(arrived + (normed,))
            normed = arrived[2]
        key_value_cells = jnp.concatenate([key_value_cells, arrived[0]], axis=0)
        query_cells = jnp.concatenate([query_cells, arrived[1]], axis=0)
    gathering = arrived[:2]
    one_pair = (one_cells, flip(after(one_cells, gathering), bits[0]))
    segment_lengths, logit_scale, kernel, _ = lax.optimization_barrier(
        (segment_lengths, logit_scale, kernel, gathering)
    )
    ends = jnp.cumsum(segment_lengths).astype(jnp.int32)

    def segment_of(positions):
        located = jnp.sum((ends[None, :] <= positions[:, None]).astype(jnp.int32), axis=1)
        return jnp.where(positions < 0, -1, located)

    scale = jnp.repeat(logit_scale * (math.log2(math.e) / HD), HD)[None, :]
    base = shard_place * local_frames
    own_positions = base + jnp.arange(local_frames, dtype=jnp.int32)
    halo_positions = jnp.concatenate(
        [base - MOST + jnp.arange(MOST), base + local_frames + jnp.arange(MOST)]
    ).astype(jnp.int32)
    own_segment, halo_segment = segment_of(own_positions), segment_of(halo_positions)
    block = tile_of(local_frames, 256)
    blocks = local_frames // block
    first_frame = base + block * jnp.arange(blocks, dtype=jnp.int32)
    last_frame = first_frame + block - 1
    low = jnp.max(jnp.where(ends[None, :] <= first_frame[:, None], ends[None, :], 0), axis=1)
    high = jnp.min(
        jnp.where(ends[None, :] > last_frame[:, None], ends[None, :], 2 * all_frames), axis=1
    )
    low, high = low - base, high - base

    def key_range(least, most, rows, offset):
        start = (jnp.clip(least, 0, rows) // LANE) * LANE
        count = jnp.maximum((most - start + KEYS - 1) // KEYS, 0)
        start = jnp.maximum(jnp.minimum(start, rows - KEYS * count), 0)
        return offset + start, count

    own_start, own_count = key_range(low, jnp.clip(high, 0, local_frames), local_frames, 0)
    before_start, before_count = key_range(
        low + MOST, jnp.where(low < 0, MOST, -KEYS), MOST, 0
    )
    after_start, after_count = key_range(
        0 * high, jnp.clip(high - local_frames, -KEYS, MOST), MOST, MOST
    )
    halo_start = jnp.where(before_count > 0, before_start, after_start)
    halo_count = jnp.where(before_count > 0, before_count, after_count)
    conv_all = conv_rows + 2 * RIM
    conv_first = base + head_place * conv_rows - RIM
    limits = jnp.concatenate([jnp.zeros((1,), jnp.int32), ends])
    limits = jnp.concatenate(
        [
            jnp.clip(limits - conv_first, 0, conv_all),
            jnp.sum((ends <= conv_first).astype(jnp.int32), keepdims=True),
            jnp.sum((limits[:-1] < conv_first + conv_all).astype(jnp.int32), keepdims=True),
        ]
    )
    taps = kernel.reshape(KERNEL * (width // LANE), LANE)

    (
        from_x, own_start, own_count, halo_start, halo_count, own_segment, halo_segment,
        limits, scale, taps,
    ) = lax.optimization_barrier(
        (
            (
                flip(key_value_cells, bits[-2]),
                flip(query_cells, other_bits[-2]),
                one_pair[1],
                two_pair[1],
            ),
            own_start, own_count, halo_start, halo_count, own_segment, halo_segment,
            limits, scale, taps,
        )
    )
    arrived = from_x[:2]
    one_pair, two_pair = (one_pair[0], from_x[2]), (two_pair[0], from_x[3])
    key_value_pieces = (key_value_cells, arrived[0])
    query_pieces = (query_cells, arrived[1])
    key_value_pieces += tuple(flip(cells, last_bit) for cells in key_value_pieces)
    query_pieces += tuple(flip(cells, last_bit) for cells in query_pieces)
    evens = jnp.reshape(even.astype(jnp.int32), (1,))
    key_value, queries, near, away = project(
        ids, alternate, evens, normed, key_value_pieces, query_pieces, scale
    )
    near = flip(near, 1)
    away = lax.ppermute(away, "tm", tm_pairs())
    upstream = all_heads(after(cotangent, queries), conv_rows)
    frame_rims = rim_pieces(after(frames, queries), 1)[0]
    frame_rows = with_rim(window_of(frames, head_place, conv_rows), frame_rims, frame_rims)

    one_cells, two_cells = join(one_pair, arrived), join(two_pair, arrived)
    one_pair = (one_cells, flip(one_cells, bits[1]))
    two_pair = (two_cells, flip(two_cells, other_bits[1]))
    for level in range(2, len(bits) - 2):
        one_cells, two_cells = join(one_pair, queries), join(two_pair, queries)
        one_pair = (one_cells, flip(one_cells, bits[level]))
        two_pair = (two_cells, flip(two_cells, other_bits[level]))
    own_sums = attend_own(own_start, own_count, queries, key_value, own_segment)
    one_cells, two_cells = join(one_pair, own_sums), join(two_pair, own_sums)
    one_pair = (one_cells, flip(one_cells, bits[-2]))
    two_pair = (two_cells, flip(two_cells, other_bits[-2]))
    heads_out = attend_rest(
        halo_start,
        halo_count,
        evens,
        queries,
        near,
        away,
        own_segment,
        halo_segment,
        own_sums,
    )
    heads_all = all_heads(after(heads_out, upstream), conv_rows)
    one_halves = one_pair + tuple(flip(after(c, heads_out), last_bit) for c in one_pair)
    two_halves = two_pair + tuple(flip(after(c, heads_out), last_bit) for c in two_pair)
    residual, gated, value, gate = open_block(
        ids, alternate, places, heads_all, frame_rows, conv_gain[None, :], one_halves, two_halves
    )
    *out_parts, depth_grad, post_sum = middle_block(
        alternate,
        places,
        limits,
        upstream,
        gated,
        residual,
        taps,
        post_gain[None, :],
        two_halves,
    )
    out_frames = in_order(send_heads(out_parts))
    glu_grad, taps_sum = spread_block(limits, depth_grad, gated, value, gate, taps)
    tap_rows = taps_sum.reshape(KERNEL, width)
    first_terms = jnp.concatenate([tap_rows, jnp.sum(post_sum, axis=0, keepdims=True)], axis=0)
    scattered = lax.all_to_all(
        first_terms.reshape(devices, (KERNEL + 1) * width // devices),
        ("head", "tm"),
        split_axis=0,
        concat_axis=0,
        tiled=True,
    )
    share = jnp.sum(scattered, axis=0)
    *grad_parts, open_sum = close_block(
        ids,
        alternate,
        places,
        upstream,
        glu_grad,
        residual,
        conv_gain[None, :],
        one_halves,
        two_halves,
    )
    grad_parts[0] = after(grad_parts[0], out_frames)
    grad_input = in_order(send_heads(grad_parts))
    last_terms = jnp.concatenate([share, jnp.sum(open_sum, axis=0)], axis=0)
    everywhere = lax.all_to_all(
        jnp.broadcast_to(last_terms[None], (devices, last_terms.shape[0])),
        ("head", "tm"),
        split_axis=0,
        concat_axis=0,
        tiled=True,
    )
    grad_scale = 1.0 / math.sqrt(all_frames)
    reduced = everywhere[:, : share.shape[0]].reshape(KERNEL + 1, width)
    open_total = jnp.sum(everywhere[:, share.shape[0] :], axis=0)
    gains = jnp.stack([open_total, reduced[KERNEL]], axis=0)
    return (out_frames, grad_input, reduced[:KERNEL] * grad_scale, gains * grad_scale)


def solution(mesh):
    placed = (
        P("tm", None),
        P(),
        P(),
        P("tm", None, "head"),
        P(None, "tm"),
        P("head"),
        P(),
        P("tm", None),
        P(),
        P(),
        P("tm", None),
        P("tm", "head"),
    )
    return jax.shard_map(
        on_device,
        mesh=mesh,
        in_specs=placed,
        out_specs=(P("tm", "head"), P("tm", "head"), P(), P()),
        check_vma=False,
    )
```
